128 devices in a mesh: seq: 32 (over x, z, core), feat: 4 (over y).
Axes of the slice: x: 4, y: 4, z: 4, core: 2. Of those that a mesh axis runs over, the one named last changes fastest.
Arguments:
- hidden: bfloat16 [16384, 1536], P('seq', 'feat'), may hold values from -24 to 24
- lengths: int32 [8], replicated, may hold values from 1 to 8192, 16384 in all
- page_table: int32 [64], replicated, may hold values from 0 to 63, each once
- first_gain: float32 [1536], replicated, may hold values from 0.5 to 1.5
- query_weight: bfloat16 [1536, 1536], P(None, 'feat'), may hold values from -0.15625 to 0.15625
- keyvalue_weight: bfloat16 [1536, 256], P(None, 'feat'), may hold values from -0.15625 to 0.15625
- output_weight: bfloat16 [1536, 1536], P('feat'), may hold values from -0.15625 to 0.15625
- second_gain: float32 [1536], replicated, may hold values from 0.5 to 1.5
- gate_weight: bfloat16 [1536, 4608], P(None, 'feat'), may hold values from -0.15625 to 0.15625
- up_weight: bfloat16 [1536, 4608], P(None, 'feat'), may hold values from -0.15625 to 0.15625
- down_weight: bfloat16 [4608, 1536], P('feat'), may hold values from -0.09375 to 0.09375
Outputs:
- output: bfloat16 [16384, 1536], P('seq', 'feat')
- cache: bfloat16 [64, 128, 256], P('seq', 'feat')
The draws below stay inside these ranges and needn't reach their ends.
Inputs may be any that keep to these rules, and one draw needn't show every extreme that they name: `lengths`: the 8 prompts fill the pack in order and sum to 16384 tokens; the longest has exactly 8192. A permutation of the 64 pages; cache block b of prompt r is page_table[r * 8 + b], and page p is held by seq index p // 2.
All inputs are finite; a program needn't handle non-finite values.
Results may differ from the reference program's by a relative error of at most 0.007.
Values may be sent and summed in bfloat16 or wider, within the bound.
No kernel may reach another device: no remote copies, remote signals or barrier semaphores. Data moves between devices by JAX's collectives and lax.ppermute only.
A program may use at most 128 MiB of HBM per device.

```python
import math
import jax
import jax.numpy as jnp
import numpy as np
from jax import lax

D = 1536
HEADS = 12
HD = 128
FF = 4608
WIN = 1024
BLK = 128
TOK_DEV = 512
TOKENS = 16384
REQS = 8
MAXLEN = 8192
WBLK = 8
PAGES = 64


def draw_hidden(key, part):
    base_key, row_key, column_key = jax.random.split(key, 3)
    base = jnp.clip(jax.random.normal(base_key, (TOKENS, D), jnp.float32), -4.0, 4.0)
    row_scale = jnp.exp(jax.random.uniform(row_key, (TOKENS, 1), jnp.float32, math.log(0.3), math.log(3.0)))
    column_scale = jnp.exp(jax.random.uniform(column_key, (1, D), jnp.float32, math.log(0.5), math.log(2.0)))
    return (base * row_scale * column_scale).astype(jnp.bfloat16)


def levels(own_key, shape, cuts, least, top_value):
    factor_of, own = 1.0, jax.random.fold_in(own_key, 6)
    for position, parts in cuts:
        heights = jnp.exp(jax.random.uniform(jax.random.fold_in(own, position), (parts,), jnp.float32, least / len(cuts), top_value / len(cuts)))
        factor_of = factor_of * jnp.repeat(heights, shape[position] // parts).reshape([-1 if axis == position else 1 for axis in range(len(shape))])
    return factor_of


def length_profile(amount, total, limit, lean):
    loads = [(1 << 20) // math.isqrt(grade ** lean) + 1 for grade in range(2, amount + 1)]
    surplus, given = total - limit - (amount - 1), [1] * (amount - 1)
    while surplus > 0:
        candidates = [i for i in range(amount - 1) if given[i] < limit]
        whole, remaining = sum([loads[i] for i in candidates]), surplus
        for i in candidates:
            addition = min(limit - given[i], max(1, remaining * loads[i] // whole), surplus)
            given[i] = given[i] + addition
            surplus = surplus - addition
    return np.array([limit] + given)


def ragged(stream_key, number_of, total, reach, skew):
    if number_of == 2:
        one = jax.random.randint(stream_key, (), max(1, total - reach), min(reach, total - 1) + 1)
        return jnp.stack([one, total - one])
    sizes = jnp.asarray(length_profile(number_of, total, reach, skew), jnp.int32)
    pairs = (number_of - 1) // 2
    giver, receiver = sizes[1:1 + 2 * pairs:2], sizes[2:2 + 2 * pairs:2]
    slack = jnp.minimum(giver - 1, reach - receiver)
    moved = jax.random.randint(jax.random.fold_in(stream_key, 1), (pairs,), 0, 1 << 20) % (slack + 1)
    sizes = sizes.at[1:1 + 2 * pairs:2].set(giver - moved).at[2:2 + 2 * pairs:2].set(receiver + moved)
    return sizes[jax.random.permutation(jax.random.fold_in(stream_key, 2), number_of)]


def scatter_about(own_key, extent, width, most, cuts=(), kind=jnp.bfloat16):
    level = levels(own_key, extent, cuts, -0.22, 0.18) if cuts else 1.0
    drawn = jax.random.normal(own_key, extent, jnp.float32) * width * level
    return jnp.minimum(jnp.maximum(drawn, -most), most).astype(kind)


def setup_inputs(seed: int = 0) -> dict:
    streams_of = jax.random.split(jax.random.key(seed), 12)
    hidden = draw_hidden(jax.random.fold_in(streams_of[11], 71), 0)
    lengths = ragged(streams_of[1], REQS, TOKENS, MAXLEN, 2).astype(jnp.int32)
    page_table = jax.random.permutation(streams_of[2], PAGES).astype(jnp.int32)
    first_gain = jnp.clip(1.0 + 0.1 * jax.random.normal(streams_of[3], (D,), jnp.float32), 0.5, 1.5)
    query_weight = scatter_about(streams_of[4], (D, D), D ** -0.5, 0.15625, ((1, 4),))
    keyvalue_weight = scatter_about(streams_of[5], (D, 2 * HD), D ** -0.5, 0.15625, ((1, 4),))
    output_weight = scatter_about(streams_of[6], (D, D), D ** -0.5, 0.15625, ((0, 4),))
    second_gain = jnp.clip(1.0 + 0.1 * jax.random.normal(streams_of[7], (D,), jnp.float32), 0.5, 1.5)
    gate_weight = scatter_about(streams_of[8], (D, FF), D ** -0.5, 0.15625, ((1, 4),))
    up_weight = scatter_about(streams_of[9], (D, FF), D ** -0.5, 0.15625, ((1, 4),))
    down_weight = scatter_about(streams_of[10], (FF, D), FF ** -0.5, 0.09375, ((0, 4),))
    return dict(hidden=hidden, lengths=lengths, page_table=page_table, first_gain=first_gain, query_weight=query_weight, keyvalue_weight=keyvalue_weight, output_weight=output_weight, second_gain=second_gain, gate_weight=gate_weight, up_weight=up_weight, down_weight=down_weight)


epsilon = 1e-06

def locate(places, lengths):
    offsets = jnp.cumsum(lengths) - lengths
    numbers = jnp.arange(lengths.shape[0], dtype=jnp.int32)
    segment = lax.optimization_barrier(jnp.sum((places[:, None] >= offsets[None, :]).astype(jnp.int32), axis=1)) - 1
    member = (segment[:, None] == numbers[None, :]).astype(jnp.int32)
    begin = lax.optimization_barrier(jnp.sum(member * offsets[None, :], axis=1))
    length = lax.optimization_barrier(jnp.sum(member * lengths[None, :], axis=1))
    return (segment, places - begin, length, begin)

def rotate(values, inner):
    half = values.shape[-1] // 2
    freq = jnp.exp(jnp.arange(half, dtype=jnp.float32) * (-2.0 * math.log(10000.0) / values.shape[-1]))
    angle = inner.astype(jnp.float32)[:, None] * freq[None, :]
    cosine = jnp.cos(angle)[:, None, :]
    sine = jnp.sin(angle)[:, None, :]
    first = values[..., :half]
    second = values[..., half:]
    return jnp.concatenate([first * cosine - second * sine, second * cosine + first * sine], axis=-1)

def normalize(values, gain):
    square = lax.optimization_barrier(jnp.sum(values * values, axis=-1, keepdims=True)) / values.shape[-1]
    return (values * lax.rsqrt(square + epsilon) * gain).astype(jnp.bfloat16)

def window_attention(block_query, block_kv, query_seg, key_seg):
    query_count = block_query.shape[0]
    key_count = block_kv.shape[0]
    head_size = block_kv.shape[1] // 2
    window = key_count - query_count
    offset = jnp.arange(key_count, dtype=jnp.int32)[None, :] - jnp.arange(query_count, dtype=jnp.int32)[:, None]
    allowed = (offset > 0) & (offset <= window) & (query_seg[:, None] == key_seg[None, :])
    scores = jnp.einsum('qhd,kd->hqk', block_query.astype(jnp.float32), block_kv[:, :head_size].astype(jnp.float32))
    scores = scores * head_size ** (-0.5)
    weights = jnp.where(allowed[None], jnp.exp(scores), 0.0)
    probs = (weights / lax.optimization_barrier(jnp.sum(weights, axis=-1, keepdims=True))).astype(jnp.bfloat16)
    mixed = jnp.einsum('hqk,kd->qhd', probs.astype(jnp.float32), block_kv[:, head_size:].astype(jnp.float32))
    return mixed.astype(jnp.bfloat16).reshape(query_count, -1)

def reference(hidden, lengths, page_table, first_gain, query_weight, keyvalue_weight, output_weight, second_gain, gate_weight, up_weight, down_weight):
    features = hidden.astype(jnp.float32)
    normed = normalize(features, first_gain)
    places = jnp.arange(TOKENS, dtype=jnp.int32)
    segment, inner, length, begin = locate(places, lengths)
    queries = jnp.dot(normed, query_weight, preferred_element_type=jnp.float32).reshape(TOKENS, HEADS, HD)
    queries = rotate(queries, inner).astype(jnp.bfloat16)
    keyvalue = jnp.dot(normed, keyvalue_weight, preferred_element_type=jnp.float32).astype(jnp.bfloat16)
    keys = rotate(keyvalue[:, None, :HD].astype(jnp.float32), inner)[:, 0, :].astype(jnp.bfloat16)
    rotated = jnp.concatenate([keys, keyvalue[:, HD:]], axis=1)
    block_rows = min(TOK_DEV, 512)
    padded = jnp.concatenate([jnp.zeros((WIN, 2 * HD), jnp.bfloat16), rotated], axis=0)
    padded_seg = jnp.concatenate([jnp.full((WIN,), -1, jnp.int32), segment], axis=0)

    def attend(index):
        first_row = (index * block_rows).astype(jnp.int32)
        block_query = lax.dynamic_slice_in_dim(queries, first_row, block_rows, 0)
        block_kv = lax.dynamic_slice_in_dim(padded, first_row, block_rows + WIN, 0)
        key_seg = lax.dynamic_slice_in_dim(padded_seg, first_row, block_rows + WIN, 0)
        query_seg = lax.dynamic_slice_in_dim(segment, first_row, block_rows, 0)
        return window_attention(block_query, block_kv, query_seg, key_seg)
    attended = lax.map(attend, jnp.arange(TOKENS // block_rows, dtype=jnp.int32)).reshape(TOKENS, D)
    residual = features + jnp.dot(attended, output_weight, preferred_element_type=jnp.float32)
    normed2 = normalize(residual, second_gain)
    gate = jnp.dot(normed2, gate_weight, preferred_element_type=jnp.float32)
    upper = jnp.dot(normed2, up_weight, preferred_element_type=jnp.float32)
    activated = (jax.nn.gelu(gate, approximate=True) * upper).astype(jnp.bfloat16)
    output = (residual + jnp.dot(activated, down_weight, preferred_element_type=jnp.float32)).astype(jnp.bfloat16)
    cached = inner >= length - WIN
    slot = inner % WIN
    page = page_table[(segment * WBLK + slot // BLK).astype(jnp.int32)]
    target = jnp.where(cached, page * BLK + slot % BLK, PAGES * BLK).astype(jnp.int32)
    cache = jnp.zeros((PAGES * BLK + 1, 2 * HD), jnp.bfloat16).at[target].set(rotated)
    cache = cache[:PAGES * BLK].reshape(PAGES, BLK, 2 * HD)
    return (output, cache)
```

```python
import functools
import math

import jax
import jax.numpy as jnp
from jax import lax
from jax.experimental import pallas as pl
from jax.experimental.pallas import tpu as pltpu
from jax.sharding import PartitionSpec as P

HD = 128
WIN = 1024
BLK = 128
epsilon = 1e-06
bf16 = jnp.bfloat16
f32 = jnp.float32
VM = pl.BlockSpec(memory_space=pltpu.VMEM)
SM = pl.BlockSpec(memory_space=pltpu.SMEM)


def from_peer(block, distance):
    n = lax.axis_size("feat")
    return lax.ppermute(block, "feat", [(i, (i - distance) % n) for i in range(n)])


def from_earlier(block, distance):
    n = lax.axis_size("seq")
    return lax.ppermute(block, "seq", [(i - distance, i) for i in range(distance, n)])


def run(body, outs, name, scalars, arrays, scratch=(), vmem=60 << 20):
    many = isinstance(outs, (list, tuple))
    return pl.pallas_call(
        body,
        out_shape=outs,
        in_specs=[SM] * len(scalars) + [VM] * len(arrays),
        out_specs=[VM] * len(outs) if many else VM,
        scratch_shapes=list(scratch),
        compiler_params=pltpu.CompilerParams(vmem_limit_bytes=vmem),
        name=name,
    )(*scalars, *arrays)


def dot(a, b):
    return jnp.dot(a, b, preferred_element_type=f32)


def norm_kv_body(place, x0, x1, x2, x3, gain, wkv, n_out, kv_out):
    f = place[0]
    xs = (x0, x1, x2, x3)
    tokens, width = x0.shape
    step = 128
    for r in range(tokens // step):
        rows = pl.ds(r * step, step)
        total = None
        for x in xs:
            v = x[rows, :].astype(f32)
            part = jnp.sum(v * v, axis=1, keepdims=True)
            total = part if total is None else total + part
        scale = lax.rsqrt(total / (width * 4) + epsilon)
        for d, x in enumerate(xs):
            g = lax.rem(f + d, 4)
            v = x[rows, :].astype(f32) * scale * gain[pl.ds(g, 1), :]
            n_out[d, rows, :] = v.astype(bf16)
    acc = None
    for d in range(4):
        g = lax.rem(f + d, 4)
        start = pl.multiple_of(g * width, 128)
        part = dot(n_out[d], wkv[pl.ds(start, width), :])
        acc = part if acc is None else acc + part
    kv = acc.astype(bf16)
    half = tokens // 2
    kv_out[...] = jnp.concatenate([kv[:half], kv[half:]], axis=1)


def query_body(place, n_in, wq, cosine, sine, q_out):
    f = place[0]
    width = n_in.shape[2]
    acc = None
    for d in range(4):
        g = lax.rem(f + d, 4)
        start = pl.multiple_of(g * width, 128)
        part = dot(n_in[d], wq[pl.ds(start, width), :])
        acc = part if acc is None else acc + part
    c = cosine[...]
    s = sine[...]
    for h in range(acc.shape[1] // HD):
        v = acc[:, h * HD : (h + 1) * HD]
        q_out[:, h * HD : (h + 1) * HD] = (v * c + pltpu.roll(v, HD // 2, 1) * s).astype(bf16)


def rotate_body(place, y0, y1, y2, y3, cosine, sine, out, hold):
    f = place[0]
    half = y0.shape[0]
    for d, y in enumerate((y0, y1, y2, y3)):
        hold[lax.rem(f + d, 4)] = y[...].astype(f32)
    for part in range(2):
        rows = pl.ds(part * half, half)
        lanes = slice(part * 64, part * 64 + 64)
        k = jnp.concatenate([hold[0][:, lanes], hold[1][:, lanes]], axis=1)
        v = jnp.concatenate([hold[2][:, lanes], hold[3][:, lanes]], axis=1)
        k = k * cosine[rows, :] + pltpu.roll(k, HD // 2, 1) * sine[rows, :]
        out[rows, :HD] = k.astype(bf16)
        out[rows, HD:] = v.astype(bf16)


def attend_body(d, place, offsets, q, far, near, own, wo, out, win, att):
    f = place[0]
    first = place[1]
    tokens = own.shape[0]
    win[pl.ds(0, tokens), :] = far[...]
    win[pl.ds(tokens, tokens), :] = near[...]
    win[pl.ds(2 * tokens, tokens), :] = own[...]
    step = 128
    b = lax.rem(f + d, 4)
    row0 = pl.multiple_of(b * step, step)
    keys = WIN + step
    k = win[pl.ds(row0, keys), :HD]
    v = win[pl.ds(row0, keys), HD:]
    pos = first + row0 + lax.broadcasted_iota(jnp.int32, (step, 1), 0)
    begin = jnp.zeros((step, 1), jnp.int32)
    for r in range(offsets.shape[0]):
        begin = jnp.where(pos >= offsets[r], offsets[r], begin)
    low = jnp.maximum(pos - (WIN - 1), begin)
    kpos = first + row0 - WIN + lax.broadcasted_iota(jnp.int32, (step, keys), 1)
    allowed = (kpos >= low) & (kpos <= pos)
    factor = HD**-0.5 * math.log2(math.e)
    for h in range(q.shape[1] // HD):
        qh = q[pl.ds(row0, step), h * HD : (h + 1) * HD]
        s = lax.dot_general(qh, k, (((1,), (1,)), ((), ())), preferred_element_type=f32)
        p = jnp.where(allowed, jnp.exp2(s * factor), 0.0)
        total = jnp.sum(p, axis=1, keepdims=True)
        mixed = dot(p.astype(bf16), v)
        att[:, h * HD : (h + 1) * HD] = (mixed / total).astype(bf16)
    out[...] = dot(att[...], wo[...]).astype(out.dtype)


def residual_body(place, x0, x1, x2, x3, p0, p1, p2, p3, gain, res_out, n_out):
    f = place[0]
    step, width = p0.shape[0], x0.shape[1]
    rows = pl.ds(pl.multiple_of(f * step, step), step)
    for d, x in enumerate((x0, x1, x2, x3)):
        res_out[lax.rem(f + d, 4)] = x[rows, :].astype(f32)
    total = None
    for g in range(4):
        cols = slice(g * width, (g + 1) * width)
        v = res_out[g] + p0[:, cols]
        v = v + p1[:, cols].astype(f32)
        v = v + p2[:, cols].astype(f32)
        v = v + p3[:, cols].astype(f32)
        res_out[g] = v
        part = jnp.sum(v * v, axis=1, keepdims=True)
        total = part if total is None else total + part
    scale = lax.rsqrt(total / (width * 4) + epsilon)
    for g in range(4):
        cols = slice(g * width, (g + 1) * width)
        n_out[:, cols] = (res_out[g] * scale * gain[:, cols]).astype(bf16)


def gelu(x):
    inner = math.sqrt(2 / math.pi) * (x + 0.044715 * (x * x * x))
    return x * (0.5 * (1.0 + jnp.tanh(inner)))


def gate_body(*refs):
    ins, (wg, wu, out) = refs[:-3], refs[-3:]
    n = jnp.concatenate([r[...] for r in ins], axis=0) if len(ins) > 1 else ins[0][...]
    chunk = 384
    for c in range(wg.shape[1] // chunk):
        cols = slice(c * chunk, (c + 1) * chunk)
        out[:, cols] = (gelu(dot(n, wg[:, cols])) * dot(n, wu[:, cols])).astype(bf16)


def down_body(d, place, a0, a13, a2, res, wd, out):
    f = place[0]
    width = out.shape[1]
    step = res.shape[1]
    g = lax.rem(f + d, 4)
    w = wd[:, pl.ds(pl.multiple_of(g * width, 128), width)]

    def rows(e):
        return pl.ds(pl.multiple_of(lax.rem(f + e, 4) * step, step), step)

    out[rows(0), :] = (dot(a0[...], w) + res[g]).astype(out.dtype)
    both = dot(a13[...], w)
    out[rows(1), :] = both[:step].astype(out.dtype)
    out[rows(3), :] = both[step:].astype(out.dtype)
    out[rows(2), :] = dot(a2[...], w).astype(out.dtype)


def image_body(target, rows, out):
    count = out.shape[0]
    step = 512
    for r in range(count // step):
        index = r * step + lax.broadcasted_iota(jnp.int32, (step, target.shape[1]), 0)
        hot = jnp.where(index == target[...], 1.0, 0.0).astype(bf16)
        out[pl.ds(r * step, step), :] = dot(hot, rows[...]).astype(bf16)


def shards(
    hidden,
    lengths,
    page_table,
    first_gain,
    query_weight,
    keyvalue_weight,
    output_weight,
    second_gain,
    gate_weight,
    up_weight,
    down_weight,
):
    tokens, width = hidden.shape
    full = width * 4
    seq_index = lax.axis_index("seq")
    f = lax.axis_index("feat")
    first = seq_index * tokens
    place = jnp.stack([f, first]).astype(jnp.int32)
    sds = jax.ShapeDtypeStruct

    x0 = hidden
    x2 = from_peer(hidden, 2)
    x1 = from_peer(hidden, 1)
    x3 = from_peer(hidden, 3)

    offsets = jnp.cumsum(lengths) - lengths
    places = first + jnp.arange(tokens, dtype=jnp.int32)
    numbers = jnp.arange(lengths.shape[0], dtype=jnp.int32)
    segment = jnp.sum((places[:, None] >= offsets[None, :]).astype(jnp.int32), axis=1) - 1
    member = (segment[:, None] == numbers[None, :]).astype(jnp.int32)
    inner = places - jnp.sum(member * offsets[None, :], axis=1)
    length = jnp.sum(member * lengths[None, :], axis=1)
    half = HD // 2
    freq = jnp.exp(jnp.arange(half, dtype=f32) * (-2.0 * math.log(10000.0) / HD))
    angle = inner.astype(f32)[:, None] * freq[None, :]
    cosine = jnp.cos(angle)
    sine = jnp.sin(angle)
    cosine = jnp.concatenate([cosine, cosine], axis=1)
    sine = jnp.concatenate([-sine, sine], axis=1)

    pages = page_table.shape[0]
    part_rows = BLK // 4
    keep = inner >= length - WIN
    slot = inner % WIN
    entry = segment * (WIN // BLK) + slot // BLK
    page = jnp.sum(
        jnp.where(
            entry[:, None] == jnp.arange(pages, dtype=jnp.int32)[None, :], page_table[None, :], 0
        ),
        axis=1,
    )
    within = slot % BLK
    mine = keep & (within // part_rows == f)
    target = jnp.where(mine, page * part_rows + within % part_rows, -1)[None, :]

    normed, kv_part = run(
        norm_kv_body,
        (sds((4, tokens, width), bf16), sds((tokens // 2, 128), bf16)),
        "norm_kv",
        [place],
        [x0, x1, x2, x3, first_gain.reshape(4, width), keyvalue_weight],
    )
    y2 = from_peer(kv_part, 2)
    y1 = from_peer(kv_part, 1)
    y3 = from_peer(kv_part, 3)
    queries = run(
        query_body,
        sds((tokens, query_weight.shape[1]), bf16),
        "queries",
        [place],
        [normed, query_weight, cosine, sine],
    )
    rotated = run(
        rotate_body,
        sds((tokens, 2 * HD), bf16),
        "rotate",
        [place],
        [kv_part, y1, y2, y3, cosine, sine],
        [pltpu.VMEM((4, tokens // 2, 128), f32)],
    )
    far = from_earlier(rotated, 2)
    near = from_earlier(rotated, 1)

    step = tokens // 4

    def attend(d, kind):
        return run(
            functools.partial(attend_body, d),
            sds((step, full), kind),
            f"attend{d}",
            [place, offsets],
            [queries, far, near, rotated, output_weight],
            [
                pltpu.VMEM((3 * tokens, 2 * HD), bf16),
                pltpu.VMEM((step, query_weight.shape[1]), bf16),
            ],
        )

    p2 = from_peer(attend(2, bf16), 2)
    p1 = from_peer(attend(1, bf16), 3)
    p3 = from_peer(attend(3, bf16), 1)
    p0 = attend(0, f32)

    image = run(image_body, sds((pages * part_rows, 2 * HD), bf16), "image", [], [target, rotated])
    image = image.reshape(32, pages // 32 * part_rows, 2 * HD)
    landed = lax.all_to_all(image, "seq", 0, 0, tiled=False)
    cache = jnp.sum(landed.astype(f32), axis=0).astype(bf16)
    cache = cache.reshape(pages // 32, part_rows, 2 * HD)

    residual, normed2 = run(
        residual_body,
        (sds((4, step, width), f32), sds((step, full), bf16)),
        "residual",
        [place],
        [x0, x1, x2, x3, p0, p1, p2, p3, second_gain.reshape(1, full)],
    )
    m1 = from_peer(normed2, 1)
    m3 = from_peer(normed2, 3)
    m2 = from_peer(normed2, 2)

    def gated(*blocks):
        return run(
            gate_body,
            sds((step * len(blocks), gate_weight.shape[1]), bf16),
            f"gate{len(blocks)}",
            [],
            [*blocks, gate_weight, up_weight],
        )

    a0 = gated(normed2)
    a13 = gated(m1, m3)
    a2 = gated(m2)

    def down(d, kind):
        return run(
            functools.partial(down_body, d),
            sds((tokens, width), kind),
            f"down{d}",
            [place],
            [a0, a13, a2, residual, down_weight],
        )

    o2 = from_peer(down(2, bf16), 2)
    o1 = from_peer(down(1, bf16), 3)
    o3 = from_peer(down(3, bf16), 1)
    o0 = down(0, f32)
    output = (o0 + o1.astype(f32) + o2.astype(f32) + o3.astype(f32)).astype(bf16)
    return (output, cache)


def solution(mesh):
    placed = (
        P("seq", "feat"),
        P(),
        P(),
        P(),
        P(None, "feat"),
        P(None, "feat"),
        P("feat", None),
        P(),
        P(None, "feat"),
        P(None, "feat"),
        P("feat", None),
    )
    return jax.shard_map(
        shards,
        mesh=mesh,
        in_specs=placed,
        out_specs=(P("seq", "feat"), P("seq", "feat", None)),
        check_vma=False,
    )
```

```python
import functools
import math

import jax
import jax.numpy as jnp
from jax import lax
from jax.experimental import pallas as pl
from jax.experimental.pallas import tpu as pltpu
from jax.sharding import PartitionSpec as P

HD = 128
WIN = 1024
BLK = 128
epsilon = 1e-06
bf16 = jnp.bfloat16
f32 = jnp.float32
VM = pl.BlockSpec(memory_space=pltpu.VMEM)
SM = pl.BlockSpec(memory_space=pltpu.SMEM)


def from_peer(block, distance):
    n = lax.axis_size("feat")
    return lax.ppermute(block, "feat", [(i, (i - distance) % n) for i in range(n)])


def from_earlier(block, distance):
    n = lax.axis_size("seq")
    return lax.ppermute(block, "seq", [(i - distance, i) for i in range(distance, n)])


def from_partner(block, bits):
    n = lax.axis_size("seq")
    return lax.ppermute(block, "seq", [(i, i ^ bits) for i in range(n)])


def run(body, outs, name, scalars, arrays, scratch=(), vmem=16 << 20):
    many = isinstance(outs, (list, tuple))
    return pl.pallas_call(
        body,
        out_shape=outs,
        in_specs=[SM] * len(scalars) + [VM] * len(arrays),
        out_specs=[VM] * len(outs) if many else VM,
        scratch_shapes=list(scratch),
        compiler_params=pltpu.CompilerParams(vmem_limit_bytes=vmem),
        cost_estimate=pl.CostEstimate(flops=2_000_000_000, transcendentals=0, bytes_accessed=10_000_000),
        name=name,
    )(*scalars, *arrays)


def dot(a, b):
    return jnp.dot(a, b, preferred_element_type=f32)


def copy_body(source, out):
    out[...] = source[...]


def merge(kept, landed, first, second):
    half = first.shape[0]
    first[...] = (kept[:half, :].astype(f32) + landed[:half, :].astype(f32)).astype(bf16)
    second[...] = (kept[half:, :].astype(f32) + landed[half:, :].astype(f32)).astype(bf16)


def norm_kv_body(place, x0, x1, x2, x3, gain, wkv, n_out, kv_out, kept):
    f = place[0]
    xs = (x0, x1, x2, x3)
    tokens, width = x0.shape
    step = 128
    for r in range(tokens // step):
        rows = pl.ds(r * step, step)
        total = None
        for x in xs:
            v = x[rows, :].astype(f32)
            part = jnp.sum(v * v, axis=1, keepdims=True)
            total = part if total is None else total + part
        scale = lax.rsqrt(total / (width * 4) + epsilon)
        for d, x in enumerate(xs):
            g = lax.rem(f + d, 4)
            v = x[rows, :].astype(f32) * scale * gain[pl.ds(g, 1), :]
            n_out[d, rows, :] = v.astype(bf16)
    own = kept.shape[1]
    own_rows = pl.ds(pl.multiple_of(f * own, own), own)
    for d, x in enumerate(xs):
        kept[lax.rem(f + d, 4)] = x[own_rows, :]
    acc = None
    for d in range(4):
        g = lax.rem(f + d, 4)
        start = pl.multiple_of(g * width, 128)
        part = dot(n_out[d], wkv[pl.ds(start, width), :])
        acc = part if acc is None else acc + part
    kv = acc.astype(bf16)
    half = tokens // 2
    kv_out[...] = jnp.concatenate([kv[:half], kv[half:]], axis=1)


def query_body(place, n_in, wq, cosine, sine, q_out):
    f = place[0]
    width = n_in.shape[2]
    acc = None
    for d in range(4):
        g = lax.rem(f + d, 4)
        start = pl.multiple_of(g * width, 128)
        part = dot(n_in[d], wq[pl.ds(start, width), :])
        acc = part if acc is None else acc + part
    c = cosine[...]
    s = sine[...]
    for h in range(acc.shape[1] // HD):
        v = acc[:, h * HD : (h + 1) * HD]
        q_out[:, h * HD : (h + 1) * HD] = (v * c + pltpu.roll(v, HD // 2, 1) * s).astype(bf16)


def rotate_body(place, y0, y1, y2, y3, cosine, sine, out, hold):
    f = place[0]
    half = y0.shape[0]
    for d, y in enumerate((y0, y1, y2, y3)):
        hold[lax.rem(f + d, 4)] = y[...].astype(f32)
    for part in range(2):
        rows = pl.ds(part * half, half)
        lanes = slice(part * 64, part * 64 + 64)
        k = jnp.concatenate([hold[0][:, lanes], hold[1][:, lanes]], axis=1)
        v = jnp.concatenate([hold[2][:, lanes], hold[3][:, lanes]], axis=1)
        k = k * cosine[rows, :] + pltpu.roll(k, HD // 2, 1) * sine[rows, :]
        out[rows, :HD] = k.astype(bf16)
        out[rows, HD:] = v.astype(bf16)


def attend_body(d, place, offsets, q, far, near, own, wo, *refs):
    if d == 0:
        merge(refs[0], refs[1], refs[3], refs[4])
        refs = refs[2:3] + refs[5:]
    out, win, att = refs
    f = place[0]
    first = place[1]
    tokens = own.shape[0]
    heads = q.shape[1] // HD
    win[pl.ds(0, tokens), :] = far[...]
    win[pl.ds(tokens, tokens), :] = near[...]
    win[pl.ds(2 * tokens, tokens), :] = own[...]
    step = 128
    b = lax.rem(f + d, 4)
    row0 = pl.multiple_of(b * step, step)
    pos = first + row0 + lax.broadcasted_iota(jnp.int32, (step, 1), 0)
    begin = jnp.zeros((step, 1), jnp.int32)
    for r in range(offsets.shape[0]):
        begin = jnp.where(pos >= offsets[r], offsets[r], begin)
    low = jnp.maximum(pos - (WIN - 1), begin)
    low = jnp.concatenate([low] * heads, axis=0)
    high = jnp.concatenate([pos] * heads, axis=0)
    qs = jnp.concatenate([q[pl.ds(row0, step), h * HD : (h + 1) * HD] for h in range(heads)], axis=0)
    factor = HD**-0.5 * math.log2(math.e)
    total = None
    mixed = None
    for start, size in ((0, 512), (512, 512), (1024, 128)):
        k = win[pl.ds(row0 + start, size), :HD]
        v = win[pl.ds(row0 + start, size), HD:]
        kpos = first + row0 + (start - WIN) + lax.broadcasted_iota(jnp.int32, (heads * step, size), 1)
        allowed = kpos >= low
        if start == WIN:
            allowed = allowed & (kpos <= high)
        s = lax.dot_general(qs, k, (((1,), (1,)), ((), ())), preferred_element_type=f32)
        p = jnp.where(allowed, jnp.exp2(s * factor), 0.0)
        part = jnp.sum(p, axis=1, keepdims=True)
        total = part if total is None else total + part
        part = dot(p.astype(bf16), v)
        mixed = part if mixed is None else mixed + part
    mixed = (mixed / total).astype(bf16)
    for h in range(heads):
        att[:, h * HD : (h + 1) * HD] = mixed[h * step : (h + 1) * step]
    out[...] = dot(att[...], wo[...]).astype(out.dtype)


def residual_body(kept, p0, p1, p2, p3, gain, rows, landed, res_out, n_out, first, second):
    merge(rows, landed, first, second)
    width = kept.shape[2]
    total = None
    for g in range(4):
        cols = slice(g * width, (g + 1) * width)
        v = kept[g].astype(f32) + p0[:, cols]
        v = v + p1[:, cols].astype(f32)
        v = v + p2[:, cols].astype(f32)
        v = v + p3[:, cols].astype(f32)
        res_out[g] = v
        part = jnp.sum(v * v, axis=1, keepdims=True)
        total = part if total is None else total + part
    scale = lax.rsqrt(total / (width * 4) + epsilon)
    for g in range(4):
        cols = slice(g * width, (g + 1) * width)
        n_out[:, cols] = (res_out[g] * scale * gain[:, cols]).astype(bf16)


def gelu(x):
    inner = math.sqrt(2 / math.pi) * (x + 0.044715 * (x * x * x))
    return x * (0.5 * (1.0 + jnp.tanh(inner)))


def feed_body(count, own, before, *refs):
    place = refs[0]
    blocks = refs[1 : 1 + count]
    refs = refs[1 + count :]
    res = earlier = None
    if own:
        merge(refs[0], refs[1], refs[-4], refs[-3])
        res, refs = refs[2], refs[3:-4] + refs[-2:]
    elif before:
        earlier, refs = refs[:3], refs[3:]
    else:
        refs[-3][...] = (refs[0][...].astype(f32) + refs[1][...].astype(f32)).astype(bf16)
        refs = refs[2:-3] + refs[-2:]
    wg, wu, wd, o0, o1, o2, o3, act, hold = refs
    f = place[0]
    rows, width = o0.shape
    n = jnp.concatenate([r[...] for r in blocks], axis=0) if count > 1 else blocks[0][...]
    chunk = 384
    for c in range(wg.shape[1] // chunk):
        cols = slice(c * chunk, (c + 1) * chunk)
        act[:, cols] = (gelu(dot(n, wg[:, cols])) * dot(n, wu[:, cols])).astype(bf16)
    for g in range(4):
        part = dot(act[...], wd[:, g * width : (g + 1) * width])
        hold[g] = part + res[g] if own else part
    o0[...] = hold[f]
    for d, o in ((1, o1), (2, o2), (3, o3)):
        lead = o.shape[0] - rows
        if before:
            o[:lead, :] = earlier[d - 1][...]
        o[lead:, :] = hold[lax.rem(f + d, 4)].astype(o.dtype)


def finish_body(place, *refs):
    ins, out, hold = refs[:-2], refs[-2], refs[-1]
    f = place[0]
    step = hold.shape[1]
    own, both, far = ins[:3]
    hold[f] = own[...]
    hold[lax.rem(f + 1, 4)] = both[:step]
    hold[lax.rem(f + 3, 4)] = both[step:]
    hold[lax.rem(f + 2, 4)] = far[...]
    for e in range(1, 4):
        early, far = ins[2 * e + 1 : 2 * e + 3]
        for row, shift in ((0, 0), (1, 1), (2, 3)):
            b = lax.rem(f + e + shift, 4)
            hold[b] = hold[b] + early[row * step : (row + 1) * step].astype(f32)
        b = lax.rem(f + e + 2, 4)
        hold[b] = hold[b] + far[...].astype(f32)
    for b in range(4):
        out[b * step : (b + 1) * step, :] = hold[b].astype(bf16)


def image_body(target, other, rows, sibling, sent, kept):
    step = sent.shape[0]
    for part, out in enumerate((sent, kept)):
        index = part * step + lax.broadcasted_iota(jnp.int32, (step, target.shape[1]), 0)
        hot = jnp.where(index == target[...], 1.0, 0.0).astype(bf16)
        total = dot(hot, rows[...])
        hot = jnp.where(index == other[...], 1.0, 0.0).astype(bf16)
        out[...] = (total + dot(hot, sibling[...])).astype(bf16)


def shards(
    hidden,
    lengths,
    page_table,
    first_gain,
    query_weight,
    keyvalue_weight,
    output_weight,
    second_gain,
    gate_weight,
    up_weight,
    down_weight,
):
    tokens, width = hidden.shape
    full = width * 4
    seq_index = lax.axis_index("seq")
    f = lax.axis_index("feat")
    first = seq_index * tokens
    place = jnp.stack([f, first]).astype(jnp.int32)
    sds = jax.ShapeDtypeStruct

    x0 = run(copy_body, sds(hidden.shape, bf16), "take_own", [], [hidden])
    x2 = from_peer(hidden, 2)
    x1 = from_peer(hidden, 1)
    x3 = from_peer(hidden, 3)

    offsets = jnp.cumsum(lengths) - lengths
    ticks = jnp.arange(tokens, dtype=jnp.int32)
    places = jnp.concatenate([first + ticks, (seq_index ^ 1) * tokens + ticks])
    numbers = jnp.arange(lengths.shape[0], dtype=jnp.int32)
    segment = jnp.sum((places[:, None] >= offsets[None, :]).astype(jnp.int32), axis=1) - 1
    member = (segment[:, None] == numbers[None, :]).astype(jnp.int32)
    inner = places - jnp.sum(member * offsets[None, :], axis=1)
    length = jnp.sum(member * lengths[None, :], axis=1)
    half = HD // 2
    freq = jnp.exp(jnp.arange(half, dtype=f32) * (-2.0 * math.log(10000.0) / HD))
    angle = inner[:tokens].astype(f32)[:, None] * freq[None, :]
    cosine = jnp.cos(angle)
    sine = jnp.sin(angle)
    cosine = jnp.concatenate([cosine, cosine], axis=1)
    sine = jnp.concatenate([-sine, sine], axis=1)

    pages = page_table.shape[0]
    part_rows = BLK // 4
    keep = inner >= length - WIN
    slot = inner % WIN
    entry = segment * (WIN // BLK) + slot // BLK
    page = jnp.sum(
        jnp.where(
            entry[:, None] == jnp.arange(pages, dtype=jnp.int32)[None, :], page_table[None, :], 0
        ),
        axis=1,
    )
    within = slot % BLK
    owner = page // 2

    def rank(mine, theirs):
        apart = mine ^ theirs
        return jnp.where(apart == 1, 0, jnp.where(apart == 2, 1, jnp.where(apart == 0, 2, 3)))

    column = rank(seq_index // 8, owner // 8) * 4 + rank(seq_index // 2 % 4, owner // 2 % 4)
    mine = keep & (within // part_rows == f) & (owner % 2 == seq_index % 2)
    target = jnp.where(mine, (column * 2 + page % 2) * part_rows + within % part_rows, -1)
    other = target[None, tokens:]
    target = target[None, :tokens]
    held_rows = 2 * part_rows

    gain1 = first_gain.reshape(4, width)
    gain2 = second_gain.reshape(1, full)
    x1, x2, x3, target, other, cosine, sine, offsets, place, gain1, gain2 = lax.optimization_barrier(
        (x1, x2, x3, target, other, cosine, sine, offsets, place, gain1, gain2)
    )
    step = tokens // 4

    normed, kv_part, kept = run(
        norm_kv_body,
        (
            sds((4, tokens, width), bf16),
            sds((tokens // 2, 128), bf16),
            sds((4, step, width), bf16),
        ),
        "norm_kv",
        [place],
        [x0, x1, x2, x3, gain1, keyvalue_weight],
    )
    y2 = from_peer(kv_part, 2)
    y1 = from_peer(kv_part, 1)
    y3 = from_peer(kv_part, 3)
    queries = run(
        query_body,
        sds((tokens, query_weight.shape[1]), bf16),
        "queries",
        [place],
        [normed, query_weight, cosine, sine],
    )
    rotated = run(
        rotate_body,
        sds((tokens, 2 * HD), bf16),
        "rotate",
        [place],
        [kv_part, y1, y2, y3, cosine, sine],
        [pltpu.VMEM((4, tokens // 2, 128), f32)],
    )
    far = from_earlier(rotated, 2)
    near = from_earlier(rotated, 1)
    sibling = from_partner(rotated, 1)
    image_sent, image_kept = run(
        image_body,
        [sds((8 * held_rows, 2 * HD), bf16)] * 2,
        "image",
        [],
        [target, other, rotated, sibling],
    )
    landed = from_partner(image_sent, 8)

    def halves(rows):
        return [sds((rows.shape[0] // 2, 2 * HD), bf16)] * 2

    queries = lax.optimization_barrier((queries, image_sent))[0]

    def attend(d, kind, cached=()):
        out = sds((step, full), kind)
        return run(
            functools.partial(attend_body, d),
            [out, *halves(cached[0])] if cached else out,
            f"attend{d}",
            [place, offsets],
            [queries, far, near, rotated, output_weight, *cached],
            [
                pltpu.VMEM((3 * tokens, 2 * HD), bf16),
                pltpu.VMEM((step, query_weight.shape[1]), bf16),
            ],
        )

    p2 = from_peer(attend(2, bf16), 2)
    p1 = from_peer(attend(1, bf16), 3)
    p3 = from_peer(attend(3, bf16), 1)
    p0, stay, go = attend(0, f32, [image_kept, landed])
    landed = from_partner(go, 24)
    residual, normed2, go, stay = run(
        residual_body,
        [sds((4, step, width), f32), sds((step, full), bf16), *halves(stay)],
        "residual",
        [],
        [kept, p0, p1, p2, p3, gain2, stay, landed],
    )
    landed = from_partner(go, 2)
    m1 = from_peer(normed2, 1)
    m3 = from_peer(normed2, 3)
    m2 = from_peer(normed2, 2)

    hidden_units = gate_weight.shape[1]

    def feed(blocks, res=(), before=(), cached=()):
        rows = step * len(blocks)
        sent = rows + (step if before else 0)
        outs = [sds((rows, width), f32)] + [sds((sent, width), bf16)] * 3
        if cached:
            outs = outs + (halves(cached[0]) if res else [sds(cached[0].shape, bf16)])
        return run(
            functools.partial(feed_body, len(blocks), bool(res), bool(before)),
            outs,
            f"feed{len(blocks)}" + ("own" if res else ""),
            [place],
            [*blocks, *cached, *res, *before, gate_weight, up_weight, down_weight],
            [pltpu.VMEM((rows, hidden_units), bf16), pltpu.VMEM((4, rows, width), f32)],
            vmem=24 << 20,
        )

    own0, *own_sent, stay, go = feed([normed2], res=[residual], cached=[stay, landed])
    landed = from_partner(go, 6)
    both0, *early = feed([m1, m3], before=own_sent)
    early = [from_peer(early[1], 2), from_peer(early[0], 3), from_peer(early[2], 1)]
    far0, *late, cache = feed([m2], cached=[stay, landed])
    late = [from_peer(late[1], 2), from_peer(late[0], 3), from_peer(late[2], 1)]
    got = [own0, both0, far0, early[2], late[2], early[0], late[0], early[1], late[1]]
    output = run(
        finish_body,
        sds((tokens, width), bf16),
        "finish",
        [place],
        got,
        [pltpu.VMEM((4, step, width), f32)],
    )
    return (output, cache.reshape(2, part_rows, 2 * HD))


def solution(mesh):
    placed = (
        P("seq", "feat"),
        P(),
        P(),
        P(),
        P(None, "feat"),
        P(None, "feat"),
        P("feat", None),
        P(),
        P(None, "feat"),
        P(None, "feat"),
        P("feat", None),
    )
    return jax.shard_map(
        shards,
        mesh=mesh,
        in_specs=placed,
        out_specs=(P("seq", "feat"), P("seq", "feat", None)),
        check_vma=False,
    )
```

```python
import functools
import math

import jax
import jax.numpy as jnp
from jax import lax
from jax.experimental import pallas as pl
from jax.experimental.pallas import tpu as pltpu
from jax.sharding import PartitionSpec as P

HD = 128
WIN = 1024
BLK = 128
epsilon = 1e-06
bf16 = jnp.bfloat16
f32 = jnp.float32
VM = pl.BlockSpec(memory_space=pltpu.VMEM)
SM = pl.BlockSpec(memory_space=pltpu.SMEM)


def from_peer(block, distance):
    n = lax.axis_size("feat")
    return lax.ppermute(block, "feat", [(i, (i - distance) % n) for i in range(n)])


def from_earlier(block, distance):
    n = lax.axis_size("seq")
    return lax.ppermute(block, "seq", [(i - distance, i) for i in range(distance, n)])


def from_partner(block, bits):
    n = lax.axis_size("seq")
    return lax.ppermute(block, "seq", [(i, i ^ bits) for i in range(n)])


def run(body, outs, name, scalars, arrays, scratch=(), vmem=16 << 20, flops=2_000_000_000):
    many = isinstance(outs, (list, tuple))
    return pl.pallas_call(
        body,
        out_shape=outs,
        in_specs=[SM] * len(scalars) + [VM] * len(arrays),
        out_specs=[VM] * len(outs) if many else VM,
        scratch_shapes=list(scratch),
        compiler_params=pltpu.CompilerParams(vmem_limit_bytes=vmem),
        cost_estimate=pl.CostEstimate(flops=flops, transcendentals=0, bytes_accessed=flops // 200),
        name=name,
    )(*scalars, *arrays)


def dot(a, b):
    return jnp.dot(a, b, preferred_element_type=f32)


def copy_body(source, out):
    out[...] = source[...]


def merge(kept, landed, first, second):
    half = first.shape[0]
    first[...] = (kept[:half, :].astype(f32) + landed[:half, :].astype(f32)).astype(bf16)
    second[...] = (kept[half:, :].astype(f32) + landed[half:, :].astype(f32)).astype(bf16)


def norm_kv_body(place, x0, x1, x2, x3, gain, wkv, n_out, kv_out, kept):
    f = place[0]
    xs = (x0, x1, x2, x3)
    tokens, width = x0.shape
    step = 128
    for r in range(tokens // step):
        rows = pl.ds(r * step, step)
        total = None
        for x in xs:
            v = x[rows, :].astype(f32)
            part = jnp.sum(v * v, axis=1, keepdims=True)
            total = part if total is None else total + part
        scale = lax.rsqrt(total / (width * 4) + epsilon)
        for d, x in enumerate(xs):
            g = lax.rem(f + d, 4)
            v = x[rows, :].astype(f32) * scale * gain[pl.ds(g, 1), :]
            n_out[d, rows, :] = v.astype(bf16)
    own = kept.shape[1]
    own_rows = pl.ds(pl.multiple_of(f * own, own), own)
    for d, x in enumerate(xs):
        kept[lax.rem(f + d, 4)] = x[own_rows, :]
    acc = None
    for d in range(4):
        g = lax.rem(f + d, 4)
        start = pl.multiple_of(g * width, 128)
        part = dot(n_out[d], wkv[pl.ds(start, width), :])
        acc = part if acc is None else acc + part
    kv = acc.astype(bf16)
    half = tokens // 2
    kv_out[...] = jnp.concatenate([kv[:half], kv[half:]], axis=1)


def query_body(place, n_in, wq, cosine, sine, q_out):
    f = place[0]
    width = n_in.shape[2]
    acc = None
    for d in range(4):
        g = lax.rem(f + d, 4)
        start = pl.multiple_of(g * width, 128)
        part = dot(n_in[d], wq[pl.ds(start, width), :])
        acc = part if acc is None else acc + part
    c = cosine[...]
    s = sine[...]
    for h in range(acc.shape[1] // HD):
        v = acc[:, h * HD : (h + 1) * HD]
        q_out[:, h * HD : (h + 1) * HD] = (v * c + pltpu.roll(v, HD // 2, 1) * s).astype(bf16)


def rotate_body(place, y0, y1, y2, y3, cosine, sine, out, hold):
    f = place[0]
    half = y0.shape[0]
    for d, y in enumerate((y0, y1, y2, y3)):
        hold[lax.rem(f + d, 4)] = y[...].astype(f32)
    for part in range(2):
        rows = pl.ds(part * half, half)
        lanes = slice(part * 64, part * 64 + 64)
        k = jnp.concatenate([hold[0][:, lanes], hold[1][:, lanes]], axis=1)
        v = jnp.concatenate([hold[2][:, lanes], hold[3][:, lanes]], axis=1)
        k = k * cosine[rows, :] + pltpu.roll(k, HD // 2, 1) * sine[rows, :]
        out[rows, :HD] = k.astype(bf16)
        out[rows, HD:] = v.astype(bf16)


def attend_body(d, place, offsets, q, far, far_other, own, other, wo, *refs):
    if d == 0:
        merge(refs[0], refs[1], refs[3], refs[4])
        refs = refs[2:3] + refs[5:]
    out, win, att = refs
    f = place[0]
    first = place[1]
    tokens = own.shape[0]
    heads = q.shape[1] // HD
    core = place[2]
    for slot, part in ((core, far), (1 - core, far_other), (2 + core, own), (3 - core, other)):
        win[pl.ds(pl.multiple_of(slot * tokens, tokens), tokens), :] = part[...]
    step = 128
    b = lax.rem(f + d, 4)
    row0 = pl.multiple_of(b * step, step)
    key0 = pl.multiple_of(core * tokens + b * step, step)
    pos = first + row0 + lax.broadcasted_iota(jnp.int32, (step, 1), 0)
    begin = jnp.zeros((step, 1), jnp.int32)
    for r in range(offsets.shape[0]):
        begin = jnp.where(pos >= offsets[r], offsets[r], begin)
    low = jnp.maximum(pos - (WIN - 1), begin)
    low = jnp.concatenate([low] * heads, axis=0)
    high = jnp.concatenate([pos] * heads, axis=0)
    qs = jnp.concatenate([q[pl.ds(row0, step), h * HD : (h + 1) * HD] for h in range(heads)], axis=0)
    factor = HD**-0.5 * math.log2(math.e)
    total = None
    mixed = None
    for start, size in ((0, 512), (512, 512), (1024, 128)):
        k = win[pl.ds(key0 + start, size), :HD]
        v = win[pl.ds(key0 + start, size), HD:]
        kpos = first + row0 + (start - WIN) + lax.broadcasted_iota(jnp.int32, (heads * step, size), 1)
        allowed = kpos >= low
        if start == WIN:
            allowed = allowed & (kpos <= high)
        s = lax.dot_general(qs, k, (((1,), (1,)), ((), ())), preferred_element_type=f32)
        p = jnp.where(allowed, jnp.exp2(s * factor), 0.0)
        part = jnp.sum(p, axis=1, keepdims=True)
        total = part if total is None else total + part
        part = dot(p.astype(bf16), v)
        mixed = part if mixed is None else mixed + part
    mixed = (mixed / total).astype(bf16)
    for h in range(heads):
        att[:, h * HD : (h + 1) * HD] = mixed[h * step : (h + 1) * step]
    out[...] = dot(att[...], wo[...]).astype(out.dtype)


def residual_body(kept, p0, p1, p2, p3, gain, rows, landed, res_out, n_out, first, second):
    merge(rows, landed, first, second)
    width = kept.shape[2]
    total = None
    for g in range(4):
        cols = slice(g * width, (g + 1) * width)
        v = kept[g].astype(f32) + p0[:, cols]
        v = v + p1[:, cols].astype(f32)
        v = v + p2[:, cols].astype(f32)
        v = v + p3[:, cols].astype(f32)
        res_out[g] = v
        part = jnp.sum(v * v, axis=1, keepdims=True)
        total = part if total is None else total + part
    scale = lax.rsqrt(total / (width * 4) + epsilon)
    for g in range(4):
        cols = slice(g * width, (g + 1) * width)
        n_out[:, cols] = (res_out[g] * scale * gain[:, cols]).astype(bf16)


def split_body(a, b, upper, lower):
    half = upper.shape[0]
    upper[...] = a[:half, :]
    lower[...] = b[half:, :]


def gelu(x):
    inner = math.sqrt(2 / math.pi) * (x + 0.044715 * (x * x * x))
    return x * (0.5 * (1.0 + jnp.tanh(inner)))


def feed_body(count, own, before, *refs):
    place = refs[0]
    blocks = refs[1 : 1 + count]
    refs = refs[1 + count :]
    res = earlier = None
    if own:
        merge(refs[0], refs[1], refs[-4], refs[-3])
        res, refs = refs[2], refs[3:-4] + refs[-2:]
    elif before:
        refs[-3][...] = (refs[0][...].astype(f32) + refs[1][...].astype(f32)).astype(bf16)
        earlier, refs = refs[2:5], refs[5:-3] + refs[-2:]
    wg, wu, wd, o0, o1, o2, o3, act, hold = refs
    f = place[0]
    rows, width = o0.shape
    n = jnp.concatenate([r[...] for r in blocks], axis=0) if count > 1 else blocks[0][...]
    chunk = 384
    for c in range(wg.shape[1] // chunk):
        cols = slice(c * chunk, (c + 1) * chunk)
        act[:, cols] = (gelu(dot(n, wg[:, cols])) * dot(n, wu[:, cols])).astype(bf16)
    for g in range(4):
        part = dot(act[...], wd[:, g * width : (g + 1) * width])
        hold[g] = part + res[g] if own else part
    o0[...] = hold[f]
    for d, o in ((1, o1), (2, o2), (3, o3)):
        lead = o.shape[0] - rows
        if before:
            o[:lead, :] = earlier[d - 1][...]
        o[lead:, :] = hold[lax.rem(f + d, 4)].astype(o.dtype)


def finish_body(place, *refs):
    ins, out, hold = refs[:-2], refs[-2], refs[-1]
    f = place[0]
    step = hold.shape[1]
    own, both, far = ins[:3]
    hold[f] = own[...]
    hold[lax.rem(f + 1, 4)] = both[:step]
    hold[lax.rem(f + 3, 4)] = both[step:]
    hold[lax.rem(f + 2, 4)] = far[...]
    for e in range(1, 4):
        early, far = ins[2 * e + 1 : 2 * e + 3]
        for row, shift in ((0, 0), (1, 1), (2, 3)):
            b = lax.rem(f + e + shift, 4)
            hold[b] = hold[b] + early[row * step : (row + 1) * step].astype(f32)
        b = lax.rem(f + e + 2, 4)
        hold[b] = hold[b] + far[...].astype(f32)
    for b in range(4):
        out[b * step : (b + 1) * step, :] = hold[b].astype(bf16)


def image_body(target, other, rows, sibling, sent, kept):
    step = sent.shape[0]
    for part, out in enumerate((sent, kept)):
        index = part * step + lax.broadcasted_iota(jnp.int32, (step, target.shape[1]), 0)
        hot = jnp.where(index == target[...], 1.0, 0.0).astype(bf16)
        total = dot(hot, rows[...])
        hot = jnp.where(index == other[...], 1.0, 0.0).astype(bf16)
        out[...] = (total + dot(hot, sibling[...])).astype(bf16)


def shards(
    hidden,
    lengths,
    page_table,
    first_gain,
    query_weight,
    keyvalue_weight,
    output_weight,
    second_gain,
    gate_weight,
    up_weight,
    down_weight,
):
    tokens, width = hidden.shape
    full = width * 4
    seq_index = lax.axis_index("seq")
    f = lax.axis_index("feat")
    first = seq_index * tokens
    place = jnp.stack([f, first, seq_index % 2]).astype(jnp.int32)
    sds = jax.ShapeDtypeStruct

    x0 = run(copy_body, sds(hidden.shape, bf16), "take_own", [], [hidden])
    x2 = from_peer(hidden, 2)
    x1 = from_peer(hidden, 1)
    x3 = from_peer(hidden, 3)

    offsets = jnp.cumsum(lengths) - lengths
    ticks = jnp.arange(tokens, dtype=jnp.int32)
    places = jnp.concatenate([first + ticks, (seq_index ^ 1) * tokens + ticks])
    numbers = jnp.arange(lengths.shape[0], dtype=jnp.int32)
    segment = jnp.sum((places[:, None] >= offsets[None, :]).astype(jnp.int32), axis=1) - 1
    member = (segment[:, None] == numbers[None, :]).astype(jnp.int32)
    inner = places - jnp.sum(member * offsets[None, :], axis=1)
    length = jnp.sum(member * lengths[None, :], axis=1)
    half = HD // 2
    freq = jnp.exp(jnp.arange(half, dtype=f32) * (-2.0 * math.log(10000.0) / HD))
    angle = inner[:tokens].astype(f32)[:, None] * freq[None, :]
    cosine = jnp.cos(angle)
    sine = jnp.sin(angle)
    cosine = jnp.concatenate([cosine, cosine], axis=1)
    sine = jnp.concatenate([-sine, sine], axis=1)

    pages = page_table.shape[0]
    part_rows = BLK // 4
    keep = inner >= length - WIN
    slot = inner % WIN
    entry = segment * (WIN // BLK) + slot // BLK
    page = jnp.sum(
        jnp.where(
            entry[:, None] == jnp.arange(pages, dtype=jnp.int32)[None, :], page_table[None, :], 0
        ),
        axis=1,
    )
    within = slot % BLK
    owner = page // 2

    def rank(mine, theirs):
        apart = mine ^ theirs
        return jnp.where(apart == 1, 0, jnp.where(apart == 2, 1, jnp.where(apart == 0, 2, 3)))

    column = rank(seq_index // 8, owner // 8) * 4 + rank(seq_index // 2 % 4, owner // 2 % 4)
    mine = keep & (within // part_rows == f) & (owner % 2 == seq_index % 2)
    target = jnp.where(mine, (column * 2 + page % 2) * part_rows + within % part_rows, -1)
    other = target[None, tokens:]
    target = target[None, :tokens]
    held_rows = 2 * part_rows

    gain1 = first_gain.reshape(4, width)
    gain2 = second_gain.reshape(1, full)
    x1, x2, x3, target, other, cosine, sine, offsets, place, gain1, gain2 = lax.optimization_barrier(
        (x1, x2, x3, target, other, cosine, sine, offsets, place, gain1, gain2)
    )
    step = tokens // 4

    normed, kv_part, kept = run(
        norm_kv_body,
        (
            sds((4, tokens, width), bf16),
            sds((tokens // 2, 128), bf16),
            sds((4, step, width), bf16),
        ),
        "norm_kv",
        [place],
        [x0, x1, x2, x3, gain1, keyvalue_weight],
    )
    y2 = from_peer(kv_part, 2)
    y1 = from_peer(kv_part, 1)
    y3 = from_peer(kv_part, 3)
    queries = run(
        query_body,
        sds((tokens, query_weight.shape[1]), bf16),
        "queries",
        [place],
        [normed, query_weight, cosine, sine],
    )
    rotated = run(
        rotate_body,
        sds((tokens, 2 * HD), bf16),
        "rotate",
        [place],
        [kv_part, y1, y2, y3, cosine, sine],
        [pltpu.VMEM((4, tokens // 2, 128), f32)],
    )
    far = from_earlier(rotated, 2)
    sibling = from_partner(rotated, 1)
    image_sent, image_kept = run(
        image_body,
        [sds((8 * held_rows, 2 * HD), bf16)] * 2,
        "image",
        [],
        [target, other, rotated, sibling],
    )
    landed = from_partner(image_sent, 8)

    def halves(rows):
        return [sds((rows.shape[0] // 2, 2 * HD), bf16)] * 2

    far, queries, _ = lax.optimization_barrier((far, queries, image_sent))
    far_other = from_partner(far, 1)

    def attend(d, kind, cached=()):
        out = sds((step, full), kind)
        return run(
            functools.partial(attend_body, d),
            [out, *halves(cached[0])] if cached else out,
            f"attend{d}",
            [place, offsets],
            [queries, far, far_other, rotated, sibling, output_weight, *cached],
            [
                pltpu.VMEM((4 * tokens, 2 * HD), bf16),
                pltpu.VMEM((step, query_weight.shape[1]), bf16),
            ],
        )

    p2 = from_peer(attend(2, bf16), 2)
    p1 = from_peer(attend(1, bf16), 3)
    p3 = from_peer(attend(3, bf16), 1)
    p0, stay, go = attend(0, f32, [image_kept, landed])
    landed = from_partner(go, 24)
    residual, normed2, go, stay = run(
        residual_body,
        [sds((4, step, width), f32), sds((step, full), bf16), *halves(stay)],
        "residual",
        [],
        [kept, p0, p1, p2, p3, gain2, stay, landed],
    )
    landed = from_partner(go, 2)
    m1 = from_peer(normed2, 1)
    m3 = from_peer(normed2, 3)
    hidden_units = gate_weight.shape[1]

    def feed(blocks, res=(), before=(), cached=()):
        rows = sum(block.shape[0] for block in blocks)
        sent = rows + (step if before else 0)
        outs = [sds((rows, width), f32)] + [sds((sent, width), bf16)] * 3
        if cached:
            outs = outs + (halves(cached[0]) if res else [sds(cached[0].shape, bf16)])
        return run(
            functools.partial(feed_body, len(blocks), bool(res), bool(before)),
            outs,
            "feed_own" if res else "feed_near" if before else "feed_far",
            [place],
            [*blocks, *cached, *res, *before, gate_weight, up_weight, down_weight],
            [pltpu.VMEM((rows, hidden_units), bf16), pltpu.VMEM((4, rows, width), f32)],
            vmem=24 << 20,
        )

    own0, *own_sent, stay, go = feed([normed2], res=[residual], cached=[stay, landed])
    landed = from_partner(go, 6)
    half_rows = step // 2
    m1, m3, _ = lax.optimization_barrier((m1, m3, own0))
    upper, lower = run(
        split_body, [sds((half_rows, full), bf16)] * 2, "split", [], [m1, m3]
    )
    m1, m3, upper, lower = lax.optimization_barrier((m1, m3, upper, lower))
    m2 = [from_peer(upper, 1), from_peer(lower, 3)]

    both0, *early, cache = feed([m1, m3], before=own_sent, cached=[stay, landed])
    early = [from_peer(early[1], 2), from_peer(early[0], 3), from_peer(early[2], 1)]
    far0, *late = feed(m2)
    late = [from_peer(late[1], 2), from_peer(late[0], 3), from_peer(late[2], 1)]
    got = [own0, both0, far0, early[2], late[2], early[0], late[0], early[1], late[1]]
    output = run(
        finish_body,
        sds((tokens, width), bf16),
        "finish",
        [place],
        got,
        [pltpu.VMEM((4, step, width), f32)],
    )
    return (output, cache.reshape(2, part_rows, 2 * HD))


def solution(mesh):
    placed = (
        P("seq", "feat"),
        P(),
        P(),
        P(),
        P(None, "feat"),
        P(None, "feat"),
        P("feat", None),
        P(),
        P(None, "feat"),
        P(None, "feat"),
        P("feat", None),
    )
    return jax.shard_map(
        shards,
        mesh=mesh,
        in_specs=placed,
        out_specs=(P("seq", "feat"), P("seq", "feat", None)),
        check_vma=False,
    )
```

```python
import functools
import math

import jax
import jax.numpy as jnp
from jax import lax
from jax.experimental import pallas as pl
from jax.experimental.pallas import tpu as pltpu
from jax.sharding import PartitionSpec as P

HD = 128
WIN = 1024
BLK = 128
epsilon = 1e-06
bf16 = jnp.bfloat16
f32 = jnp.float32
VM = pl.BlockSpec(memory_space=pltpu.VMEM)
SM = pl.BlockSpec(memory_space=pltpu.SMEM)


def from_peer(block, distance):
    n = lax.axis_size("feat")
    return lax.ppermute(block, "feat", [(i, (i - distance) % n) for i in range(n)])


def from_earlier(block, distance):
    n = lax.axis_size("seq")
    return lax.ppermute(block, "seq", [(i - distance, i) for i in range(distance, n)])


def from_partner(block, bits):
    n = lax.axis_size("seq")
    return lax.ppermute(block, "seq", [(i, i ^ bits) for i in range(n)])


def run(body, outs, name, scalars, arrays, scratch=(), vmem=16 << 20, flops=2_000_000_000):
    many = isinstance(outs, (list, tuple))
    return pl.pallas_call(
        body,
        out_shape=outs,
        in_specs=[SM] * len(scalars) + [VM] * len(arrays),
        out_specs=[VM] * len(outs) if many else VM,
        scratch_shapes=list(scratch),
        compiler_params=pltpu.CompilerParams(vmem_limit_bytes=vmem),
        cost_estimate=pl.CostEstimate(flops=flops, transcendentals=0, bytes_accessed=flops // 200),
        name=name,
    )(*scalars, *arrays)


def dot(a, b):
    return jnp.dot(a, b, preferred_element_type=f32)


def copy_body(source, out):
    out[...] = source[...]


def merge(kept, landed, first, second):
    half = first.shape[0]
    first[...] = (kept[:half, :].astype(f32) + landed[:half, :].astype(f32)).astype(bf16)
    second[...] = (kept[half:, :].astype(f32) + landed[half:, :].astype(f32)).astype(bf16)


def norm_kv_body(place, x0, x1, x2, x3, gain, wkv, n_out, kv_out, kept):
    f = place[0]
    xs = (x0, x1, x2, x3)
    tokens, width = x0.shape
    step = 128
    for r in range(tokens // step):
        rows = pl.ds(r * step, step)
        total = None
        for x in xs:
            v = x[rows, :].astype(f32)
            part = jnp.sum(v * v, axis=1, keepdims=True)
            total = part if total is None else total + part
        scale = lax.rsqrt(total / (width * 4) + epsilon)
        for d, x in enumerate(xs):
            g = lax.rem(f + d, 4)
            v = x[rows, :].astype(f32) * scale * gain[pl.ds(g, 1), :]
            n_out[d, rows, :] = v.astype(bf16)
    own = kept.shape[1]
    own_rows = pl.ds(pl.multiple_of(f * own, own), own)
    for d, x in enumerate(xs):
        kept[lax.rem(f + d, 4)] = x[own_rows, :]
    acc = None
    for d in range(4):
        g = lax.rem(f + d, 4)
        start = pl.multiple_of(g * width, 128)
        part = dot(n_out[d], wkv[pl.ds(start, width), :])
        acc = part if acc is None else acc + part
    kv = acc.astype(bf16)
    half = tokens // 2
    kv_out[...] = jnp.concatenate([kv[:half], kv[half:]], axis=1)


def query_body(place, n_in, wq, cosine, sine, q_out):
    f = place[0]
    width = n_in.shape[2]
    acc = None
    for d in range(4):
        g = lax.rem(f + d, 4)
        start = pl.multiple_of(g * width, 128)
        part = dot(n_in[d], wq[pl.ds(start, width), :])
        acc = part if acc is None else acc + part
    factor = HD**-0.5 * math.log2(math.e)
    c = cosine[: acc.shape[0], :] * factor
    s = sine[: acc.shape[0], :] * factor
    for h in range(acc.shape[1] // HD):
        v = acc[:, h * HD : (h + 1) * HD]
        q_out[:, h * HD : (h + 1) * HD] = (v * c + pltpu.roll(v, HD // 2, 1) * s).astype(bf16)


def join_body(a, b, out):
    half = a.shape[0]
    out[:half, :] = a[...]
    out[half:, :] = b[...]


def rotate_body(place, y0, y1, y2, y3, cosine, sine, out, hold):
    f = place[0]
    for d, y in enumerate((y0, y1, y2, y3)):
        hold[lax.rem(f + d, 4)] = y[...].astype(f32)
    quarter = y0.shape[0] // 2
    for block in range(4):
        source = slice(block // 2 * quarter, block // 2 * quarter + quarter)
        lanes = slice(block % 2 * 64, block % 2 * 64 + 64)
        rows = pl.ds(block * quarter, quarter)
        k = jnp.concatenate([hold[0, source, lanes], hold[1, source, lanes]], axis=1)
        v = jnp.concatenate([hold[2, source, lanes], hold[3, source, lanes]], axis=1)
        k = k * cosine[rows, :] + pltpu.roll(k, HD // 2, 1) * sine[rows, :]
        out[rows, :HD] = k.astype(bf16)
        out[rows, HD:] = v.astype(bf16)


def attend_body(d, place, offsets, q, mine, theirs, wo, *refs):
    if d == 0:
        merge(refs[0], refs[1], refs[3], refs[4])
        refs = refs[2:3] + refs[5:]
    out, win, att = refs
    f = place[0]
    first = place[1]
    tokens = q.shape[0]
    heads = q.shape[1] // HD
    core = place[2]
    for slot, part, row in ((core, mine, 1), (1 - core, theirs, 1), (2 + core, mine, 0), (3 - core, theirs, 0)):
        rows = pl.ds(pl.multiple_of(slot * tokens, tokens), tokens)
        win[rows, :] = part[row * tokens : (row + 1) * tokens, :]
    step = 128
    b = lax.rem(f + d, 4)
    row0 = pl.multiple_of(b * step, step)
    key0 = pl.multiple_of(core * tokens + b * step, step)
    pos = first + row0 + lax.broadcasted_iota(jnp.int32, (step, 1), 0)
    begin = jnp.zeros((step, 1), jnp.int32)
    for r in range(offsets.shape[0]):
        begin = jnp.where(pos >= offsets[r], offsets[r], begin)
    low = jnp.maximum(pos - (WIN - 1), begin)
    low = jnp.concatenate([low] * heads, axis=0)
    high = jnp.concatenate([pos] * heads, axis=0)
    qs = jnp.concatenate([q[pl.ds(row0, step), h * HD : (h + 1) * HD] for h in range(heads)], axis=0)
    total = None
    mixed = None
    for start, size in ((0, 512), (512, 512), (1024, 128)):
        k = win[pl.ds(key0 + start, size), :HD]
        v = win[pl.ds(key0 + start, size), HD:]
        kpos = first + row0 + (start - WIN) + lax.broadcasted_iota(jnp.int32, (heads * step, size), 1)
        allowed = kpos >= low
        if start == WIN:
            allowed = allowed & (kpos <= high)
        s = lax.dot_general(qs, k, (((1,), (1,)), ((), ())), preferred_element_type=f32)
        p = jnp.where(allowed, jnp.exp2(s), 0.0)
        part = jnp.sum(p, axis=1, keepdims=True)
        total = part if total is None else total + part
        part = dot(p.astype(bf16), v)
        mixed = part if mixed is None else mixed + part
    mixed = (mixed / total).astype(bf16)
    for h in range(heads):
        att[:, h * HD : (h + 1) * HD] = mixed[h * step : (h + 1) * step]
    out[...] = dot(att[...], wo[...]).astype(out.dtype)


def residual_body(kept, p0, p1, p2, p3, gain, rows, landed, res_out, n_out, first, second):
    merge(rows, landed, first, second)
    width = kept.shape[2]
    total = None
    for g in range(4):
        cols = slice(g * width, (g + 1) * width)
        v = kept[g].astype(f32) + p0[:, cols]
        v = v + p1[:, cols].astype(f32)
        v = v + p2[:, cols].astype(f32)
        v = v + p3[:, cols].astype(f32)
        res_out[g] = v
        part = jnp.sum(v * v, axis=1, keepdims=True)
        total = part if total is None else total + part
    scale = lax.rsqrt(total / (width * 4) + epsilon)
    for g in range(4):
        cols = slice(g * width, (g + 1) * width)
        n_out[:, cols] = (res_out[g] * scale * gain[:, cols]).astype(bf16)


def split_body(a, b, upper, lower):
    half = upper.shape[0]
    upper[...] = a[:half, :]
    lower[...] = b[half:, :]


def gelu(x):
    inner = math.sqrt(2 / math.pi) * (x + 0.044715 * (x * x * x))
    return x * (0.5 * (1.0 + jnp.tanh(inner)))


def feed_body(count, own, before, *refs):
    place = refs[0]
    blocks = refs[1 : 1 + count]
    refs = refs[1 + count :]
    res = earlier = None
    if own:
        merge(refs[0], refs[1], refs[-4], refs[-3])
        res, refs = refs[2], refs[3:-4] + refs[-2:]
    elif before:
        refs[-3][...] = (refs[0][...].astype(f32) + refs[1][...].astype(f32)).astype(bf16)
        earlier, refs = refs[2:5], refs[5:-3] + refs[-2:]
    wg, wu, wd, o0, o1, o2, o3, act, hold = refs
    f = place[0]
    rows, width = o0.shape
    n = jnp.concatenate([r[...] for r in blocks], axis=0) if count > 1 else blocks[0][...]
    chunk = 512
    for c in range(0, wg.shape[1], chunk):
        cols = slice(c, min(c + chunk, wg.shape[1]))
        act[:, cols] = (gelu(dot(n, wg[:, cols])) * dot(n, wu[:, cols])).astype(bf16)
    for g in (0, 2):
        pair = dot(act[...], wd[:, g * width : (g + 2) * width])
        for h in (0, 1):
            part = pair[:, h * width : (h + 1) * width]
            hold[g + h] = part + res[g + h] if own else part
    o0[...] = hold[f]
    for d, o in ((1, o1), (2, o2), (3, o3)):
        lead = o.shape[0] - rows
        if before:
            o[:lead, :] = earlier[d - 1][...]
        o[lead:, :] = hold[lax.rem(f + d, 4)].astype(o.dtype)


def finish_body(place, *refs):
    ins, out = refs[:-1], refs[-1]
    f = place[0]
    step = out.shape[0] // 4
    own, both, far = ins[:3]
    for r in range(4):
        total = (own[...], both[:step], far[...], both[step:])[r]
        for e in range(1, 4):
            early, late = ins[2 * e + 1 : 2 * e + 3]
            shift = (r - e) % 4
            if shift == 2:
                piece = late[...]
            else:
                row = (0, 1, None, 2)[shift] * step
                piece = early[row : row + step]
            total = total + piece.astype(f32)
        rows = pl.ds(pl.multiple_of(lax.rem(f + r, 4) * step, step), step)
        out[rows, :] = total.astype(bf16)


def image_body(target, other, rows, sibling, sent, kept):
    step = sent.shape[0]
    for part, out in enumerate((sent, kept)):
        index = part * step + lax.broadcasted_iota(jnp.int32, (step, target.shape[1]), 0)
        hot = jnp.where(index == target[...], 1.0, 0.0).astype(bf16)
        count = target.shape[1]
        total = dot(hot, rows[:count, :])
        hot = jnp.where(index == other[...], 1.0, 0.0).astype(bf16)
        out[...] = (total + dot(hot, sibling[:count, :])).astype(bf16)


def shards(
    hidden,
    lengths,
    page_table,
    first_gain,
    query_weight,
    keyvalue_weight,
    output_weight,
    second_gain,
    gate_weight,
    up_weight,
    down_weight,
):
    tokens, width = hidden.shape
    full = width * 4
    seq_index = lax.axis_index("seq")
    f = lax.axis_index("feat")
    first = seq_index * tokens
    place = jnp.stack([f, first, seq_index % 2]).astype(jnp.int32)
    sds = jax.ShapeDtypeStruct

    x0 = run(copy_body, sds(hidden.shape, bf16), "take_own", [], [hidden])
    x2 = from_peer(hidden, 2)
    x1 = from_peer(hidden, 1)
    x3 = from_peer(hidden, 3)

    offsets = jnp.cumsum(lengths) - lengths
    ticks = jnp.arange(tokens, dtype=jnp.int32)
    places = jnp.concatenate([first + ticks, first - WIN + ticks, (seq_index ^ 1) * tokens + ticks])
    numbers = jnp.arange(lengths.shape[0], dtype=jnp.int32)
    segment = jnp.sum((places[:, None] >= offsets[None, :]).astype(jnp.int32), axis=1) - 1
    member = (segment[:, None] == numbers[None, :]).astype(jnp.int32)
    inner = places - jnp.sum(member * offsets[None, :], axis=1)
    length = jnp.sum(member * lengths[None, :], axis=1)
    half = HD // 2
    freq = jnp.exp(jnp.arange(half, dtype=f32) * (-2.0 * math.log(10000.0) / HD))
    angle = inner[: 2 * tokens].astype(f32)[:, None] * freq[None, :]
    cosine = jnp.cos(angle)
    sine = jnp.sin(angle)
    cosine = jnp.concatenate([cosine, cosine], axis=1)
    sine = jnp.concatenate([-sine, sine], axis=1)

    pages = page_table.shape[0]
    part_rows = BLK // 4
    keep = inner >= length - WIN
    slot = inner % WIN
    entry = segment * (WIN // BLK) + slot // BLK
    page = jnp.sum(
        jnp.where(
            entry[:, None] == jnp.arange(pages, dtype=jnp.int32)[None, :], page_table[None, :], 0
        ),
        axis=1,
    )
    within = slot % BLK
    owner = page // 2

    def rank(mine, theirs):
        apart = mine ^ theirs
        return jnp.where(apart == 1, 0, jnp.where(apart == 2, 1, jnp.where(apart == 0, 2, 3)))

    column = rank(seq_index // 8, owner // 8) * 4 + rank(seq_index // 2 % 4, owner // 2 % 4)
    mine = keep & (within // part_rows == f) & (owner % 2 == seq_index % 2)
    target = jnp.where(mine, (column * 2 + page % 2) * part_rows + within % part_rows, -1)
    other = target[None, 2 * tokens :]
    target = target[None, :tokens]
    held_rows = 2 * part_rows

    gain1 = first_gain.reshape(4, width)
    gain2 = second_gain.reshape(1, full)
    x1, x2, x3, target, other, cosine, sine, offsets, place, gain1, gain2 = lax.optimization_barrier(
        (x1, x2, x3, target, other, cosine, sine, offsets, place, gain1, gain2)
    )
    step = tokens // 4

    normed, kv_part, kept = run(
        norm_kv_body,
        (
            sds((4, tokens, width), bf16),
            sds((tokens // 2, 128), bf16),
            sds((4, step, width), bf16),
        ),
        "norm_kv",
        [place],
        [x0, x1, x2, x3, gain1, keyvalue_weight],
    )
    far_part = from_earlier(kv_part, 2)
    queries = run(
        query_body,
        sds((tokens, query_weight.shape[1]), bf16),
        "queries",
        [place],
        [normed, query_weight, cosine, sine],
    )
    far_part, queries = lax.optimization_barrier((far_part, queries))
    y0 = run(join_body, sds((tokens, 128), bf16), "join", [], [kv_part, far_part])
    y2, y1, y3 = from_peer(y0, 2), from_peer(y0, 1), from_peer(y0, 3)
    mine = run(
        rotate_body,
        sds((2 * tokens, 2 * HD), bf16),
        "rotate",
        [place],
        [y0, y1, y2, y3, cosine, sine],
        [pltpu.VMEM((4, tokens, 128), f32)],
    )
    theirs = from_partner(mine, 1)
    def halves(rows):
        return [sds((rows.shape[0] // 2, 2 * HD), bf16)] * 2

    def attend(d, kind, cached=()):
        out = sds((step, full), kind)
        return run(
            functools.partial(attend_body, d),
            [out, *halves(cached[0])] if cached else out,
            f"attend{d}",
            [place, offsets],
            [queries, mine, theirs, output_weight, *cached],
            [
                pltpu.VMEM((4 * tokens, 2 * HD), bf16),
                pltpu.VMEM((step, query_weight.shape[1]), bf16),
            ],
        )

    s2 = attend(2, bf16)
    p2 = from_peer(s2, 2)
    image_sent, image_kept = run(
        image_body,
        [sds((8 * held_rows, 2 * HD), bf16)] * 2,
        "image",
        [],
        [target, other, mine, theirs],
    )
    landed = from_partner(image_sent, 8)

    p1 = from_peer(attend(1, bf16), 3)
    p3 = from_peer(attend(3, bf16), 1)
    p0, stay, go = attend(0, f32, [image_kept, landed])
    landed = from_partner(go, 24)
    residual, normed2, go, stay = run(
        residual_body,
        [sds((4, step, width), f32), sds((step, full), bf16), *halves(stay)],
        "residual",
        [],
        [kept, p0, p2, p1, p3, gain2, stay, landed],
    )
    landed = from_partner(go, 2)
    m1 = from_peer(normed2, 1)
    m3 = from_peer(normed2, 3)
    hidden_units = gate_weight.shape[1]

    def feed(blocks, res=(), before=(), cached=()):
        rows = sum(block.shape[0] for block in blocks)
        sent = rows + (step if before else 0)
        outs = [sds((rows, width), f32)] + [sds((sent, width), bf16)] * 3
        if cached:
            outs = outs + (halves(cached[0]) if res else [sds(cached[0].shape, bf16)])
        return run(
            functools.partial(feed_body, len(blocks), bool(res), bool(before)),
            outs,
            "feed_own" if res else "feed_near" if before else "feed_far",
            [place],
            [*blocks, *cached, *res, *before, gate_weight, up_weight, down_weight],
            [pltpu.VMEM((rows, hidden_units), bf16), pltpu.VMEM((4, rows, width), f32)],
            vmem=24 << 20,
        )

    own0, *own_sent, stay, go = feed([normed2], res=[residual], cached=[stay, landed])
    landed = from_partner(go, 6)
    half_rows = step // 2
    m1, m3, _ = lax.optimization_barrier((m1, m3, own0))
    upper, lower = run(
        split_body, [sds((half_rows, full), bf16)] * 2, "split", [], [m1, m3]
    )
    m1, m3, upper, lower = lax.optimization_barrier((m1, m3, upper, lower))
    m2 = [from_peer(upper, 1), from_peer(lower, 3)]

    both0, *early, cache = feed([m1, m3], before=own_sent, cached=[stay, landed])
    early = [from_peer(early[1], 2), from_peer(early[0], 3), from_peer(early[2], 1)]
    far0, *late = feed(m2)
    late = [from_peer(late[1], 2), from_peer(late[0], 3), from_peer(late[2], 1)]
    got = [own0, both0, far0, early[2], late[2], early[0], late[0], early[1], late[1]]
    output = run(
        finish_body,
        sds((tokens, width), bf16),
        "finish",
        [place],
        got,
    )
    return (output, cache.reshape(2, part_rows, 2 * HD))


def solution(mesh):
    placed = (
        P("seq", "feat"),
        P(),
        P(),
        P(),
        P(None, "feat"),
        P(None, "feat"),
        P("feat", None),
        P(),
        P(None, "feat"),
        P(None, "feat"),
        P("feat", None),
    )
    return jax.shard_map(
        shards,
        mesh=mesh,
        in_specs=placed,
        out_specs=(P("seq", "feat"), P("seq", "feat", None)),
        check_vma=False,
    )
```

```python
import functools
import math

import jax
import jax.numpy as jnp
from jax import lax
from jax.experimental import pallas as pl
from jax.experimental.pallas import tpu as pltpu
from jax.sharding import PartitionSpec as P

HD = 128
WIN = 1024
BLK = 128
epsilon = 1e-06
bf16 = jnp.bfloat16
f32 = jnp.float32
VM = pl.BlockSpec(memory_space=pltpu.VMEM)
SM = pl.BlockSpec(memory_space=pltpu.SMEM)


def from_peer(block, distance):
    n = lax.axis_size("feat")
    return lax.ppermute(block, "feat", [(i, (i - distance) % n) for i in range(n)])


def from_earlier(block, distance):
    n = lax.axis_size("seq")
    return lax.ppermute(block, "seq", [(i - distance, i) for i in range(distance, n)])


def from_partner(block, bits):
    n = lax.axis_size("seq")
    return lax.ppermute(block, "seq", [(i, i ^ bits) for i in range(n)])


def run(body, outs, name, scalars, arrays, scratch=(), vmem=16 << 20, flops=2_000_000_000):
    many = isinstance(outs, (list, tuple))
    return pl.pallas_call(
        body,
        out_shape=outs,
        in_specs=[SM] * len(scalars) + [VM] * len(arrays),
        out_specs=[VM] * len(outs) if many else VM,
        scratch_shapes=list(scratch),
        compiler_params=pltpu.CompilerParams(vmem_limit_bytes=vmem),
        cost_estimate=pl.CostEstimate(flops=flops, transcendentals=0, bytes_accessed=flops // 200),
        name=name,
    )(*scalars, *arrays)


def dot(a, b):
    return jnp.dot(a, b, preferred_element_type=f32)


def copy_body(source, out):
    out[...] = source[...]


def merge(kept, landed, first, second):
    half = first.shape[0]
    first[...] = (kept[:half, :].astype(f32) + landed[:half, :].astype(f32)).astype(bf16)
    second[...] = (kept[half:, :].astype(f32) + landed[half:, :].astype(f32)).astype(bf16)


def norm_kv_body(place, x0, x1, x2, x3, gain, wkv, n_out, kv_out, kept):
    f = place[0]
    xs = (x0, x1, x2, x3)
    tokens, width = x0.shape
    step = 128
    for r in range(tokens // step):
        rows = pl.ds(r * step, step)
        total = None
        for x in xs:
            v = x[rows, :].astype(f32)
            part = jnp.sum(v * v, axis=1, keepdims=True)
            total = part if total is None else total + part
        scale = lax.rsqrt(total / (width * 4) + epsilon)
        for d, x in enumerate(xs):
            g = lax.rem(f + d, 4)
            v = x[rows, :].astype(f32) * scale * gain[pl.ds(g, 1), :]
            n_out[d, rows, :] = v.astype(bf16)
    own = kept.shape[1]
    own_rows = pl.ds(pl.multiple_of(f * own, own), own)
    for d, x in enumerate(xs):
        kept[lax.rem(f + d, 4)] = x[own_rows, :]
    acc = None
    for d in range(4):
        g = lax.rem(f + d, 4)
        start = pl.multiple_of(g * width, 128)
        part = dot(n_out[d], wkv[pl.ds(start, width), :])
        acc = part if acc is None else acc + part
    kv = acc.astype(bf16)
    half = tokens // 2
    kv_out[...] = jnp.concatenate([kv[:half], kv[half:]], axis=1)


def query_body(place, n_in, wq, cosine, sine, q_out):
    f = place[0]
    width = n_in.shape[2]
    acc = None
    for d in range(4):
        g = lax.rem(f + d, 4)
        start = pl.multiple_of(g * width, 128)
        part = dot(n_in[d], wq[pl.ds(start, width), :])
        acc = part if acc is None else acc + part
    factor = HD**-0.5 * math.log2(math.e)
    c = cosine[: acc.shape[0], :] * factor
    s = sine[: acc.shape[0], :] * factor
    for h in range(acc.shape[1] // HD):
        v = acc[:, h * HD : (h + 1) * HD]
        q_out[:, h * HD : (h + 1) * HD] = (v * c + pltpu.roll(v, HD // 2, 1) * s).astype(bf16)


def join_body(a, b, out):
    half = a.shape[0]
    out[:half, :] = a[...]
    out[half:, :] = b[...]


def rotate_body(place, y0, y1, y2, y3, cosine, sine, out, hold):
    f = place[0]
    for d, y in enumerate((y0, y1, y2, y3)):
        hold[lax.rem(f + d, 4)] = y[...].astype(f32)
    quarter = y0.shape[0] // 2
    for block in range(4):
        source = slice(block // 2 * quarter, block // 2 * quarter + quarter)
        lanes = slice(block % 2 * 64, block % 2 * 64 + 64)
        rows = pl.ds(block * quarter, quarter)
        k = jnp.concatenate([hold[0, source, lanes], hold[1, source, lanes]], axis=1)
        v = jnp.concatenate([hold[2, source, lanes], hold[3, source, lanes]], axis=1)
        k = k * cosine[rows, :] + pltpu.roll(k, HD // 2, 1) * sine[rows, :]
        out[rows, :HD] = k.astype(bf16)
        out[rows, HD:] = v.astype(bf16)


def attend_body(d, place, offsets, q, mine, theirs, wo, *refs):
    if d == 0:
        merge(refs[0], refs[1], refs[3], refs[4])
        refs = refs[2:3] + refs[5:]
    out, win, att = refs
    f = place[0]
    first = place[1]
    tokens = q.shape[0]
    heads = q.shape[1] // HD
    core = place[2]
    for slot, part, row in ((core, mine, 1), (1 - core, theirs, 1), (2 + core, mine, 0), (3 - core, theirs, 0)):
        rows = pl.ds(pl.multiple_of(slot * tokens, tokens), tokens)
        win[rows, :] = part[row * tokens : (row + 1) * tokens, :]
    step = 128
    b = lax.rem(f + d, 4)
    row0 = pl.multiple_of(b * step, step)
    key0 = pl.multiple_of(core * tokens + b * step, step)
    pos = first + row0 + lax.broadcasted_iota(jnp.int32, (step, 1), 0)
    begin = jnp.zeros((step, 1), jnp.int32)
    for r in range(offsets.shape[0]):
        begin = jnp.where(pos >= offsets[r], offsets[r], begin)
    low = jnp.maximum(pos - (WIN - 1), begin)
    low = jnp.concatenate([low] * heads, axis=0)
    high = jnp.concatenate([pos] * heads, axis=0)
    qs = jnp.concatenate([q[pl.ds(row0, step), h * HD : (h + 1) * HD] for h in range(heads)], axis=0)
    total = None
    mixed = None
    for start, size in ((0, 512), (512, 512), (1024, 128)):
        k = win[pl.ds(key0 + start, size), :HD]
        v = win[pl.ds(key0 + start, size), HD:]
        kpos = first + row0 + (start - WIN) + lax.broadcasted_iota(jnp.int32, (heads * step, size), 1)
        allowed = kpos >= low
        if start == WIN:
            allowed = allowed & (kpos <= high)
        s = lax.dot_general(qs, k, (((1,), (1,)), ((), ())), preferred_element_type=f32)
        p = jnp.where(allowed, jnp.exp2(s), 0.0)
        part = jnp.sum(p, axis=1, keepdims=True)
        total = part if total is None else total + part
        part = dot(p.astype(bf16), v)
        mixed = part if mixed is None else mixed + part
    mixed = (mixed / total).astype(bf16)
    for h in range(heads):
        att[:, h * HD : (h + 1) * HD] = mixed[h * step : (h + 1) * step]
    out[...] = dot(att[...], wo[...]).astype(out.dtype)


def residual_body(kept, p0, p1, p2, p3, gain, rows, landed, res_out, n_out, first, second):
    merge(rows, landed, first, second)
    width = kept.shape[2]
    total = None
    for g in range(4):
        cols = slice(g * width, (g + 1) * width)
        v = kept[g].astype(f32) + p0[:, cols]
        v = v + p1[:, cols].astype(f32)
        v = v + p2[:, cols].astype(f32)
        v = v + p3[:, cols].astype(f32)
        res_out[g] = v
        part = jnp.sum(v * v, axis=1, keepdims=True)
        total = part if total is None else total + part
    scale = lax.rsqrt(total / (width * 4) + epsilon)
    for g in range(4):
        cols = slice(g * width, (g + 1) * width)
        n_out[:, cols] = (res_out[g] * scale * gain[:, cols]).astype(bf16)


def split_body(a, b, upper, lower):
    half = upper.shape[0]
    upper[...] = a[:half, :]
    lower[...] = b[half:, :]


def gelu(x):
    inner = math.sqrt(2 / math.pi) * (x + 0.044715 * (x * x * x))
    return x * (0.5 * (1.0 + jnp.tanh(inner)))


def feed_body(count, own, before, cached, *refs):
    place = refs[0]
    blocks = refs[1 : 1 + count]
    refs = refs[1 + count :]
    if cached:
        outs, (act, hold) = refs[-2 - cached : -2], refs[-2:]
        if own:
            merge(refs[0], refs[1], *outs)
        else:
            outs[0][...] = (refs[0][...].astype(f32) + refs[1][...].astype(f32)).astype(bf16)
        refs = refs[2 : -2 - cached] + (act, hold)
    res = None
    if own:
        res, refs = refs[0], refs[1:]
    earlier = dict(zip(before, refs[: len(before)]))
    wg, wu, wd, o0, o1, o2, o3, act, hold = refs[len(before) :]
    f = place[0]
    rows, width = o0.shape
    n = jnp.concatenate([r[...] for r in blocks], axis=0) if count > 1 else blocks[0][...]
    chunk = 512
    for c in range(0, wg.shape[1], chunk):
        cols = slice(c, min(c + chunk, wg.shape[1]))
        act[:, cols] = (gelu(dot(n, wg[:, cols])) * dot(n, wu[:, cols])).astype(bf16)
    for g in (0, 2):
        pair = dot(act[...], wd[:, g * width : (g + 2) * width])
        for h in (0, 1):
            part = pair[:, h * width : (h + 1) * width]
            hold[g + h] = part + res[g + h] if own else part
    o0[...] = hold[f]
    for d, o in ((1, o1), (2, o2), (3, o3)):
        lead = o.shape[0] - rows
        if d in earlier:
            o[:lead, :] = earlier[d][...]
        o[lead:, :] = hold[lax.rem(f + d, 4)].astype(o.dtype)


def early_sum_body(own, both, far, early2, early3, out):
    step = own.shape[0]
    for r in range(4):
        total = (own[...], both[:step], far[...], both[step:])[r]
        for e, early in ((2, early2), (3, early3)):
            shift = (r - e) % 4
            if shift != 2:
                row = (0, 1, None, 2)[shift] * step
                total = total + early[row : row + step].astype(f32)
        out[r] = total


def finish_body(place, some, late2, late3, whole, out):
    f = place[0]
    step = some.shape[1]
    for r in range(4):
        row = (0, 1, 3, 2)[(r - 1) % 4] * step
        total = some[r] + whole[row : row + step].astype(f32)
        if r < 2:
            total = total + (late2, late3)[r][...].astype(f32)
        rows = pl.ds(pl.multiple_of(lax.rem(f + r, 4) * step, step), step)
        out[rows, :] = total.astype(bf16)


def image_body(target, other, rows, sibling, sent, kept):
    step = sent.shape[0]
    for part, out in enumerate((sent, kept)):
        index = part * step + lax.broadcasted_iota(jnp.int32, (step, target.shape[1]), 0)
        hot = jnp.where(index == target[...], 1.0, 0.0).astype(bf16)
        count = target.shape[1]
        total = dot(hot, rows[:count, :])
        hot = jnp.where(index == other[...], 1.0, 0.0).astype(bf16)
        out[...] = (total + dot(hot, sibling[:count, :])).astype(bf16)


def shards(
    hidden,
    lengths,
    page_table,
    first_gain,
    query_weight,
    keyvalue_weight,
    output_weight,
    second_gain,
    gate_weight,
    up_weight,
    down_weight,
):
    tokens, width = hidden.shape
    full = width * 4
    seq_index = lax.axis_index("seq")
    f = lax.axis_index("feat")
    first = seq_index * tokens
    place = jnp.stack([f, first, seq_index % 2]).astype(jnp.int32)
    sds = jax.ShapeDtypeStruct

    x0 = run(copy_body, sds(hidden.shape, bf16), "take_own", [], [hidden])
    x2 = from_peer(hidden, 2)
    x1 = from_peer(hidden, 1)
    x3 = from_peer(hidden, 3)

    offsets = jnp.cumsum(lengths) - lengths
    ticks = jnp.arange(tokens, dtype=jnp.int32)
    places = jnp.concatenate([first + ticks, first - WIN + ticks, (seq_index ^ 1) * tokens + ticks])
    numbers = jnp.arange(lengths.shape[0], dtype=jnp.int32)
    segment = jnp.sum((places[:, None] >= offsets[None, :]).astype(jnp.int32), axis=1) - 1
    member = (segment[:, None] == numbers[None, :]).astype(jnp.int32)
    inner = places - jnp.sum(member * offsets[None, :], axis=1)
    length = jnp.sum(member * lengths[None, :], axis=1)
    half = HD // 2
    freq = jnp.exp(jnp.arange(half, dtype=f32) * (-2.0 * math.log(10000.0) / HD))
    angle = inner[: 2 * tokens].astype(f32)[:, None] * freq[None, :]
    cosine = jnp.cos(angle)
    sine = jnp.sin(angle)
    cosine = jnp.concatenate([cosine, cosine], axis=1)
    sine = jnp.concatenate([-sine, sine], axis=1)

    pages = page_table.shape[0]
    part_rows = BLK // 4
    keep = inner >= length - WIN
    slot = inner % WIN
    entry = segment * (WIN // BLK) + slot // BLK
    page = jnp.sum(
        jnp.where(
            entry[:, None] == jnp.arange(pages, dtype=jnp.int32)[None, :], page_table[None, :], 0
        ),
        axis=1,
    )
    within = slot % BLK
    owner = page // 2

    def rank(mine, theirs):
        apart = mine ^ theirs
        return jnp.where(apart == 1, 0, jnp.where(apart == 2, 1, jnp.where(apart == 0, 2, 3)))

    column = rank(seq_index // 8, owner // 8) * 4 + rank(seq_index // 2 % 4, owner // 2 % 4)
    mine = keep & (within // part_rows == f) & (owner % 2 == seq_index % 2)
    target = jnp.where(mine, (column * 2 + page % 2) * part_rows + within % part_rows, -1)
    other = target[None, 2 * tokens :]
    target = target[None, :tokens]
    held_rows = 2 * part_rows

    gain1 = first_gain.reshape(4, width)
    gain2 = second_gain.reshape(1, full)
    x1, x2, x3, target, other, cosine, sine, offsets, place, gain1, gain2 = lax.optimization_barrier(
        (x1, x2, x3, target, other, cosine, sine, offsets, place, gain1, gain2)
    )
    step = tokens // 4

    normed, kv_part, kept = run(
        norm_kv_body,
        (
            sds((4, tokens, width), bf16),
            sds((tokens // 2, 128), bf16),
            sds((4, step, width), bf16),
        ),
        "norm_kv",
        [place],
        [x0, x1, x2, x3, gain1, keyvalue_weight],
    )
    far_part = from_earlier(kv_part, 2)
    queries = run(
        query_body,
        sds((tokens, query_weight.shape[1]), bf16),
        "queries",
        [place],
        [normed, query_weight, cosine, sine],
    )
    far_part, queries = lax.optimization_barrier((far_part, queries))
    y0 = run(join_body, sds((tokens, 128), bf16), "join", [], [kv_part, far_part])
    y2, y1, y3 = from_peer(y0, 2), from_peer(y0, 1), from_peer(y0, 3)
    mine = run(
        rotate_body,
        sds((2 * tokens, 2 * HD), bf16),
        "rotate",
        [place],
        [y0, y1, y2, y3, cosine, sine],
        [pltpu.VMEM((4, tokens, 128), f32)],
    )
    theirs = from_partner(mine, 1)
    def halves(rows):
        return [sds((rows.shape[0] // 2, 2 * HD), bf16)] * 2

    def attend(d, kind, cached=()):
        out = sds((step, full), kind)
        return run(
            functools.partial(attend_body, d),
            [out, *halves(cached[0])] if cached else out,
            f"attend{d}",
            [place, offsets],
            [queries, mine, theirs, output_weight, *cached],
            [
                pltpu.VMEM((4 * tokens, 2 * HD), bf16),
                pltpu.VMEM((step, query_weight.shape[1]), bf16),
            ],
        )

    s2 = attend(2, bf16)
    p2 = from_peer(s2, 2)
    image_sent, image_kept = run(
        image_body,
        [sds((8 * held_rows, 2 * HD), bf16)] * 2,
        "image",
        [],
        [target, other, mine, theirs],
    )
    landed = from_partner(image_sent, 8)

    p1 = from_peer(attend(1, bf16), 3)
    p3 = from_peer(attend(3, bf16), 1)
    p0, stay, go = attend(0, f32, [image_kept, landed])
    landed = from_partner(go, 24)
    residual, normed2, go, stay = run(
        residual_body,
        [sds((4, step, width), f32), sds((step, full), bf16), *halves(stay)],
        "residual",
        [],
        [kept, p0, p2, p1, p3, gain2, stay, landed],
    )
    landed = from_partner(go, 2)
    m1 = from_peer(normed2, 1)
    m3 = from_peer(normed2, 3)
    hidden_units = gate_weight.shape[1]

    def feed(name, blocks, res=(), before=(), cached=()):
        rows = sum(block.shape[0] for block in blocks)
        lead = {d: rows_before.shape[0] for d, rows_before in before}
        outs = [sds((rows, width), f32)]
        outs += [sds((rows + lead.get(d, 0), width), bf16) for d in (1, 2, 3)]
        more = []
        if cached:
            more = halves(cached[0]) if res else [sds(cached[0].shape, bf16)]
        return run(
            functools.partial(feed_body, len(blocks), bool(res), tuple(lead), len(more)),
            outs + more,
            name,
            [place],
            [*blocks, *cached, *res, *(b for _, b in before), gate_weight, up_weight, down_weight],
            [pltpu.VMEM((rows, hidden_units), bf16), pltpu.VMEM((4, rows, width), f32)],
            vmem=24 << 20,
        )

    own0, *own_sent, stay, go = feed("feed_own", [normed2], res=[residual], cached=[stay, landed])
    landed = from_partner(go, 6)
    half_rows = step // 2
    m1, m3, _ = lax.optimization_barrier((m1, m3, own0))
    upper, lower = run(
        split_body, [sds((half_rows, full), bf16)] * 2, "split", [], [m1, m3]
    )
    m1, m3, upper, lower = lax.optimization_barrier((m1, m3, upper, lower))
    m2 = [from_peer(upper, 1), from_peer(lower, 3)]

    both0, early1, early2, early3, cache = feed(
        "feed_near", [m1, m3], before=list(zip((1, 2, 3), own_sent)), cached=[stay, landed]
    )
    early2 = from_peer(early2, 2)
    early1 = from_peer(early1, 3)
    far0, late1, late2, whole = feed("feed_far", m2, before=[(3, early3)])
    whole = from_peer(whole, 1)
    late2 = from_peer(late2, 2)
    late1 = from_peer(late1, 3)
    some = run(
        early_sum_body,
        sds((4, step, width), f32),
        "early_sum",
        [],
        [own0, both0, far0, early2, early1],
        flops=10_000_000_000,
    )
    output = run(
        finish_body,
        sds((tokens, width), bf16),
        "finish",
        [place],
        [some, late2, late1, whole],
    )
    return (output, cache.reshape(2, part_rows, 2 * HD))


def solution(mesh):
    placed = (
        P("seq", "feat"),
        P(),
        P(),
        P(),
        P(None, "feat"),
        P(None, "feat"),
        P("feat", None),
        P(),
        P(None, "feat"),
        P(None, "feat"),
        P("feat", None),
    )
    return jax.shard_map(
        shards,
        mesh=mesh,
        in_specs=placed,
        out_specs=(P("seq", "feat"), P("seq", "feat", None)),
        check_vma=False,
    )
```

```python
import functools
import math

import jax
import jax.numpy as jnp
from jax import lax
from jax.experimental import pallas as pl
from jax.experimental.pallas import tpu as pltpu
from jax.sharding import PartitionSpec as P

HD = 128
WIN = 1024
BLK = 128
epsilon = 1e-06
bf16 = jnp.bfloat16
f32 = jnp.float32
VM = pl.BlockSpec(memory_space=pltpu.VMEM)
SM = pl.BlockSpec(memory_space=pltpu.SMEM)


def from_peer(block, distance):
    n = lax.axis_size("feat")
    return lax.ppermute(block, "feat", [(i, (i - distance) % n) for i in range(n)])


def from_earlier(block, distance):
    n = lax.axis_size("seq")
    return lax.ppermute(block, "seq", [(i - distance, i) for i in range(distance, n)])


def to_side(block, distances):
    n, m = lax.axis_size("seq"), lax.axis_size("feat")
    route = [(i * m + j, i * m + (j + distances[i % 2]) % m) for i in range(n) for j in range(m)]
    return lax.ppermute(block, ("seq", "feat"), route)


def from_partner(block, bits):
    n = lax.axis_size("seq")
    return lax.ppermute(block, "seq", [(i, i ^ bits) for i in range(n)])


def run(body, outs, name, scalars, arrays, scratch=(), vmem=16 << 20, flops=2_000_000_000):
    many = isinstance(outs, (list, tuple))
    return pl.pallas_call(
        body,
        out_shape=outs,
        in_specs=[SM] * len(scalars) + [VM] * len(arrays),
        out_specs=[VM] * len(outs) if many else VM,
        scratch_shapes=list(scratch),
        compiler_params=pltpu.CompilerParams(vmem_limit_bytes=vmem),
        cost_estimate=pl.CostEstimate(flops=flops, transcendentals=0, bytes_accessed=flops // 200),
        name=name,
    )(*scalars, *arrays)


def dot(a, b):
    return jnp.dot(a, b, preferred_element_type=f32)


def copy_body(source, out):
    out[...] = source[...]


def merge(kept, landed, first, second):
    half = first.shape[0]
    first[...] = (kept[:half, :].astype(f32) + landed[:half, :].astype(f32)).astype(bf16)
    second[...] = (kept[half:, :].astype(f32) + landed[half:, :].astype(f32)).astype(bf16)


def norm_kv_body(place, x0, x1, x2, x3, gain, wkv, n_out, kv_out, kept):
    f = place[0]
    xs = (x0, x1, x2, x3)
    tokens, width = x0.shape
    step = 128
    for r in range(tokens // step):
        rows = pl.ds(r * step, step)
        total = None
        for x in xs:
            v = x[rows, :].astype(f32)
            part = jnp.sum(v * v, axis=1, keepdims=True)
            total = part if total is None else total + part
        scale = lax.rsqrt(total / (width * 4) + epsilon)
        for d, x in enumerate(xs):
            g = lax.rem(f + d, 4)
            v = x[rows, :].astype(f32) * scale * gain[pl.ds(g, 1), :]
            n_out[d, rows, :] = v.astype(bf16)
    own = kept.shape[1]
    own_rows = pl.ds(pl.multiple_of(f * own, own), own)
    for d, x in enumerate(xs):
        kept[lax.rem(f + d, 4)] = x[own_rows, :]
    acc = None
    for d in range(4):
        g = lax.rem(f + d, 4)
        start = pl.multiple_of(g * width, 128)
        part = dot(n_out[d], wkv[pl.ds(start, width), :])
        acc = part if acc is None else acc + part
    kv = acc.astype(bf16)
    half = tokens // 2
    kv_out[...] = jnp.concatenate([kv[:half], kv[half:]], axis=1)


def query_body(place, n_in, wq, cosine, sine, q_out):
    f = place[0]
    width = n_in.shape[2]
    acc = None
    for d in range(4):
        g = lax.rem(f + d, 4)
        start = pl.multiple_of(g * width, 128)
        part = dot(n_in[d], wq[pl.ds(start, width), :])
        acc = part if acc is None else acc + part
    factor = HD**-0.5 * math.log2(math.e)
    c = cosine[: acc.shape[0], :] * factor
    s = sine[: acc.shape[0], :] * factor
    for h in range(acc.shape[1] // HD):
        v = acc[:, h * HD : (h + 1) * HD]
        q_out[:, h * HD : (h + 1) * HD] = (v * c + pltpu.roll(v, HD // 2, 1) * s).astype(bf16)


def join_body(a, b, out):
    half = a.shape[0]
    out[:half, :] = a[...]
    out[half:, :] = b[...]


def rotate_body(place, y0, y1, y2, y3, cosine, sine, out, hold):
    f = place[0]
    for d, y in enumerate((y0, y1, y2, y3)):
        hold[lax.rem(f + d, 4)] = y[...].astype(f32)
    quarter = y0.shape[0] // 2
    for block in range(4):
        source = slice(block // 2 * quarter, block // 2 * quarter + quarter)
        lanes = slice(block % 2 * 64, block % 2 * 64 + 64)
        rows = pl.ds(block * quarter, quarter)
        k = jnp.concatenate([hold[0, source, lanes], hold[1, source, lanes]], axis=1)
        v = jnp.concatenate([hold[2, source, lanes], hold[3, source, lanes]], axis=1)
        k = k * cosine[rows, :] + pltpu.roll(k, HD // 2, 1) * sine[rows, :]
        out[rows, :HD] = k.astype(bf16)
        out[rows, HD:] = v.astype(bf16)


def attend_body(d, place, offsets, q, mine, theirs, wo, *refs):
    if d == 0:
        merge(refs[0], refs[1], refs[3], refs[4])
        refs = refs[2:3] + refs[5:]
    out, win, att = refs
    f = place[0]
    first = place[1]
    tokens = q.shape[0]
    heads = q.shape[1] // HD
    core = place[2]
    for slot, part, row in ((core, mine, 1), (1 - core, theirs, 1), (2 + core, mine, 0), (3 - core, theirs, 0)):
        rows = pl.ds(pl.multiple_of(slot * tokens, tokens), tokens)
        win[rows, :] = part[row * tokens : (row + 1) * tokens, :]
    step = 128
    b = lax.rem(f + d, 4)
    row0 = pl.multiple_of(b * step, step)
    key0 = pl.multiple_of(core * tokens + b * step, step)
    pos = first + row0 + lax.broadcasted_iota(jnp.int32, (step, 1), 0)
    begin = jnp.zeros((step, 1), jnp.int32)
    for r in range(offsets.shape[0]):
        begin = jnp.where(pos >= offsets[r], offsets[r], begin)
    low = jnp.maximum(pos - (WIN - 1), begin)
    low = jnp.concatenate([low] * heads, axis=0)
    high = jnp.concatenate([pos] * heads, axis=0)
    qs = jnp.concatenate([q[pl.ds(row0, step), h * HD : (h + 1) * HD] for h in range(heads)], axis=0)
    total = None
    mixed = None
    for start, size in ((0, 512), (512, 512), (1024, 128)):
        k = win[pl.ds(key0 + start, size), :HD]
        v = win[pl.ds(key0 + start, size), HD:]
        kpos = first + row0 + (start - WIN) + lax.broadcasted_iota(jnp.int32, (heads * step, size), 1)
        allowed = kpos >= low
        if start == WIN:
            allowed = allowed & (kpos <= high)
        s = lax.dot_general(qs, k, (((1,), (1,)), ((), ())), preferred_element_type=f32)
        p = jnp.where(allowed, jnp.exp2(s), 0.0)
        part = jnp.sum(p, axis=1, keepdims=True)
        total = part if total is None else total + part
        part = dot(p.astype(bf16), v)
        mixed = part if mixed is None else mixed + part
    mixed = (mixed / total).astype(bf16)
    for h in range(heads):
        att[:, h * HD : (h + 1) * HD] = mixed[h * step : (h + 1) * step]
    out[...] = dot(att[...], wo[...]).astype(out.dtype)


def residual_body(kept, p0, p1, p2, p3, gain, rows, landed, res_out, n_out, first, second):
    merge(rows, landed, first, second)
    width = kept.shape[2]
    total = None
    for g in range(4):
        cols = slice(g * width, (g + 1) * width)
        v = kept[g].astype(f32) + p0[:, cols]
        v = v + p1[:, cols].astype(f32)
        v = v + p2[:, cols].astype(f32)
        v = v + p3[:, cols].astype(f32)
        res_out[g] = v
        part = jnp.sum(v * v, axis=1, keepdims=True)
        total = part if total is None else total + part
    scale = lax.rsqrt(total / (width * 4) + epsilon)
    for g in range(4):
        cols = slice(g * width, (g + 1) * width)
        n_out[:, cols] = (res_out[g] * scale * gain[:, cols]).astype(bf16)


def pick_body(place, ahead, behind, out):
    @pl.when(place[2] == 0)
    def _():
        out[...] = behind[...]

    @pl.when(place[2] == 1)
    def _():
        out[...] = ahead[...]


def gelu(x):
    inner = math.sqrt(2 / math.pi) * (x + 0.044715 * (x * x * x))
    return x * (0.5 * (1.0 + jnp.tanh(inner)))


def feed_body(count, own, before, cached, *refs):
    place = refs[0]
    blocks = refs[1 : 1 + count]
    refs = refs[1 + count :]
    if cached:
        outs, (act, hold) = refs[-2 - cached : -2], refs[-2:]
        if own:
            merge(refs[0], refs[1], *outs)
        else:
            outs[0][...] = (refs[0][...].astype(f32) + refs[1][...].astype(f32)).astype(bf16)
        refs = refs[2 : -2 - cached] + (act, hold)
    res = None
    if own:
        res, refs = refs[0], refs[1:]
    earlier = dict(zip(before, refs[: len(before)]))
    wg, wu, wd, o0, o1, o2, o3, act, hold = refs[len(before) :]
    f = place[0]
    rows, width = o0.shape
    n = jnp.concatenate([r[...] for r in blocks], axis=0) if count > 1 else blocks[0][...]
    chunk = 512
    for c in range(0, wg.shape[1], chunk):
        cols = slice(c, min(c + chunk, wg.shape[1]))
        act[:, cols] = (gelu(dot(n, wg[:, cols])) * dot(n, wu[:, cols])).astype(bf16)
    for g in (0, 2):
        pair = dot(act[...], wd[:, g * width : (g + 2) * width])
        for h in (0, 1):
            part = pair[:, h * width : (h + 1) * width]
            hold[g + h] = part + res[g + h] if own else part
    o0[...] = hold[f]
    for d, o in ((1, o1), (2, o2), (3, o3)):
        lead = o.shape[0] - rows
        if d in earlier:
            o[:lead, :] = earlier[d][...]
        target = d if d == 2 else d + (2 - d) * 2 * place[2]
        o[lead:, :] = hold[lax.rem(f + target, 4)].astype(o.dtype)


def early_sum_body(place, own, both, far, early2, early1, out):
    step = own.shape[0]
    out[0] = own[...]
    out[1] = both[:step]
    out[2] = far[...]
    out[3] = both[step:]
    side = 3 - 2 * place[2]
    for row, shift in enumerate((0, 1, 3)):
        rows = slice(row * step, row * step + step)
        r = (shift + 2) % 4
        out[r] = out[r] + early2[rows].astype(f32)
        r = lax.rem(shift + side, 4)
        out[r] = out[r] + early1[rows].astype(f32)


def finish_body(place, some, late2, late1, whole, out):
    f, core = place[0], place[2]
    step = some.shape[1]
    side = 1 + 2 * core
    for row, shift in enumerate((0, 1, 3, 2)):
        r = lax.rem(shift + side, 4)
        total = some[r] + whole[row * step : row * step + step].astype(f32)
        if shift == 0:
            total = total + late1[...].astype(f32)
        elif shift != 2:
            mine = core == (0 if shift == 3 else 1)
            total = total + jnp.where(mine, late2[...].astype(f32), 0.0)
        rows = pl.ds(pl.multiple_of(lax.rem(f + r, 4) * step, step), step)
        out[rows, :] = total.astype(bf16)


def image_body(target, other, rows, sibling, sent, kept):
    step = sent.shape[0]
    for part, out in enumerate((sent, kept)):
        index = part * step + lax.broadcasted_iota(jnp.int32, (step, target.shape[1]), 0)
        hot = jnp.where(index == target[...], 1.0, 0.0).astype(bf16)
        count = target.shape[1]
        total = dot(hot, rows[:count, :])
        hot = jnp.where(index == other[...], 1.0, 0.0).astype(bf16)
        out[...] = (total + dot(hot, sibling[:count, :])).astype(bf16)


def shards(
    hidden,
    lengths,
    page_table,
    first_gain,
    query_weight,
    keyvalue_weight,
    output_weight,
    second_gain,
    gate_weight,
    up_weight,
    down_weight,
):
    tokens, width = hidden.shape
    full = width * 4
    seq_index = lax.axis_index("seq")
    f = lax.axis_index("feat")
    first = seq_index * tokens
    place = jnp.stack([f, first, seq_index % 2]).astype(jnp.int32)
    sds = jax.ShapeDtypeStruct

    x0 = run(copy_body, sds(hidden.shape, bf16), "take_own", [], [hidden])
    x2 = from_peer(hidden, 2)
    x1 = from_peer(hidden, 1)
    x3 = from_peer(hidden, 3)

    offsets = jnp.cumsum(lengths) - lengths
    ticks = jnp.arange(tokens, dtype=jnp.int32)
    places = jnp.concatenate([first + ticks, first - WIN + ticks, (seq_index ^ 1) * tokens + ticks])
    numbers = jnp.arange(lengths.shape[0], dtype=jnp.int32)
    segment = jnp.sum((places[:, None] >= offsets[None, :]).astype(jnp.int32), axis=1) - 1
    member = (segment[:, None] == numbers[None, :]).astype(jnp.int32)
    inner = places - jnp.sum(member * offsets[None, :], axis=1)
    length = jnp.sum(member * lengths[None, :], axis=1)
    half = HD // 2
    freq = jnp.exp(jnp.arange(half, dtype=f32) * (-2.0 * math.log(10000.0) / HD))
    angle = inner[: 2 * tokens].astype(f32)[:, None] * freq[None, :]
    cosine = jnp.cos(angle)
    sine = jnp.sin(angle)
    cosine = jnp.concatenate([cosine, cosine], axis=1)
    sine = jnp.concatenate([-sine, sine], axis=1)

    pages = page_table.shape[0]
    part_rows = BLK // 4
    keep = inner >= length - WIN
    slot = inner % WIN
    entry = segment * (WIN // BLK) + slot // BLK
    page = jnp.sum(
        jnp.where(
            entry[:, None] == jnp.arange(pages, dtype=jnp.int32)[None, :], page_table[None, :], 0
        ),
        axis=1,
    )
    within = slot % BLK
    owner = page // 2

    def rank(mine, theirs):
        apart = mine ^ theirs
        return jnp.where(apart == 1, 0, jnp.where(apart == 2, 1, jnp.where(apart == 0, 2, 3)))

    column = rank(seq_index // 8, owner // 8) * 4 + rank(seq_index // 2 % 4, owner // 2 % 4)
    mine = keep & (within // part_rows == f) & (owner % 2 == seq_index % 2)
    target = jnp.where(mine, (column * 2 + page % 2) * part_rows + within % part_rows, -1)
    other = target[None, 2 * tokens :]
    target = target[None, :tokens]
    held_rows = 2 * part_rows

    gain1 = first_gain.reshape(4, width)
    gain2 = second_gain.reshape(1, full)
    x1, x2, x3, target, other, cosine, sine, offsets, place, gain1, gain2 = lax.optimization_barrier(
        (x1, x2, x3, target, other, cosine, sine, offsets, place, gain1, gain2)
    )
    step = tokens // 4

    normed, kv_part, kept = run(
        norm_kv_body,
        (
            sds((4, tokens, width), bf16),
            sds((tokens // 2, 128), bf16),
            sds((4, step, width), bf16),
        ),
        "norm_kv",
        [place],
        [x0, x1, x2, x3, gain1, keyvalue_weight],
    )
    far_part = from_earlier(kv_part, 2)
    queries = run(
        query_body,
        sds((tokens, query_weight.shape[1]), bf16),
        "queries",
        [place],
        [normed, query_weight, cosine, sine],
    )
    far_part, queries = lax.optimization_barrier((far_part, queries))
    y0 = run(join_body, sds((tokens, 128), bf16), "join", [], [kv_part, far_part])
    y2, y1, y3 = from_peer(y0, 2), from_peer(y0, 1), from_peer(y0, 3)
    mine = run(
        rotate_body,
        sds((2 * tokens, 2 * HD), bf16),
        "rotate",
        [place],
        [y0, y1, y2, y3, cosine, sine],
        [pltpu.VMEM((4, tokens, 128), f32)],
    )
    theirs = from_partner(mine, 1)
    def halves(rows):
        return [sds((rows.shape[0] // 2, 2 * HD), bf16)] * 2

    def attend(d, kind, cached=()):
        out = sds((step, full), kind)
        return run(
            functools.partial(attend_body, d),
            [out, *halves(cached[0])] if cached else out,
            f"attend{d}",
            [place, offsets],
            [queries, mine, theirs, output_weight, *cached],
            [
                pltpu.VMEM((4 * tokens, 2 * HD), bf16),
                pltpu.VMEM((step, query_weight.shape[1]), bf16),
            ],
        )

    s2 = attend(2, bf16)
    p2 = from_peer(s2, 2)
    image_sent, image_kept = run(
        image_body,
        [sds((8 * held_rows, 2 * HD), bf16)] * 2,
        "image",
        [],
        [target, other, mine, theirs],
    )
    landed = from_partner(image_sent, 8)

    p1 = from_peer(attend(1, bf16), 3)
    p3 = from_peer(attend(3, bf16), 1)
    p0, stay, go = attend(0, f32, [image_kept, landed])
    landed = from_partner(go, 24)
    residual, normed2, go, stay = run(
        residual_body,
        [sds((4, step, width), f32), sds((step, full), bf16), *halves(stay)],
        "residual",
        [],
        [kept, p0, p2, p1, p3, gain2, stay, landed],
    )
    landed = from_partner(go, 2)
    m1 = from_peer(normed2, 1)
    m3 = from_peer(normed2, 3)
    hidden_units = gate_weight.shape[1]

    def feed(name, blocks, res=(), before=(), cached=()):
        rows = sum(block.shape[0] for block in blocks)
        lead = {d: rows_before.shape[0] for d, rows_before in before}
        outs = [sds((rows, width), f32)]
        outs += [sds((rows + lead.get(d, 0), width), bf16) for d in (1, 2, 3)]
        more = []
        if cached:
            more = halves(cached[0]) if res else [sds(cached[0].shape, bf16)]
        return run(
            functools.partial(feed_body, len(blocks), bool(res), tuple(lead), len(more)),
            outs + more,
            name,
            [place],
            [*blocks, *cached, *res, *(b for _, b in before), gate_weight, up_weight, down_weight],
            [pltpu.VMEM((rows, hidden_units), bf16), pltpu.VMEM((4, rows, width), f32)],
            vmem=24 << 20,
            flops=20_000_000_000 if before and cached else 2_000_000_000,
        )

    own0, *own_sent, stay, go = feed("feed_own", [normed2], res=[residual], cached=[stay, landed])
    landed = from_partner(go, 6)
    m1, m3, _ = lax.optimization_barrier((m1, m3, own0))
    passed = run(pick_body, sds((step, full), bf16), "pick", [place], [m1, m3])
    m1, m3, passed = lax.optimization_barrier((m1, m3, passed))
    m2 = to_side(passed, (1, 3))
    both0, early1, early2, early3, cache = feed(
        "feed_near", [m1, m3], before=list(zip((1, 2, 3), own_sent)), cached=[stay, landed]
    )
    early2 = from_peer(early2, 2)
    early1 = to_side(early1, (1, 3))
    far0, late1, late2, whole = feed("feed_far", [m2], before=[(3, early3)])
    whole = to_side(whole, (3, 1))
    late2 = from_peer(late2, 2)
    late1 = to_side(late1, (1, 3))
    some = run(
        early_sum_body,
        sds((4, step, width), f32),
        "early_sum",
        [place],
        [own0, both0, far0, early2, early1],
        flops=10_000_000_000,
    )
    output = run(
        finish_body,
        sds((tokens, width), bf16),
        "finish",
        [place],
        [some, late2, late1, whole],
    )
    return (output, cache.reshape(2, part_rows, 2 * HD))


def solution(mesh):
    placed = (
        P("seq", "feat"),
        P(),
        P(),
        P(),
        P(None, "feat"),
        P(None, "feat"),
        P("feat", None),
        P(),
        P(None, "feat"),
        P(None, "feat"),
        P("feat", None),
    )
    return jax.shard_map(
        shards,
        mesh=mesh,
        in_specs=placed,
        out_specs=(P("seq", "feat"), P("seq", "feat", None)),
        check_vma=False,
    )
```

```python
import functools
import math

import jax
import jax.numpy as jnp
from jax import lax
from jax.experimental import pallas as pl
from jax.experimental.pallas import tpu as pltpu
from jax.sharding import PartitionSpec as P

HD = 128
WIN = 1024
BLK = 128
epsilon = 1e-06
bf16 = jnp.bfloat16
f32 = jnp.float32
VM = pl.BlockSpec(memory_space=pltpu.VMEM)
SM = pl.BlockSpec(memory_space=pltpu.SMEM)


def from_peer(block, distance):
    n = lax.axis_size("feat")
    return lax.ppermute(block, "feat", [(i, (i - distance) % n) for i in range(n)])


def from_earlier(block, distance):
    n = lax.axis_size("seq")
    return lax.ppermute(block, "seq", [(i - distance, i) for i in range(distance, n)])


def to_side(block, distances):
    n, m = lax.axis_size("seq"), lax.axis_size("feat")
    route = [(i * m + j, i * m + (j + distances[i % 2]) % m) for i in range(n) for j in range(m)]
    return lax.ppermute(block, ("seq", "feat"), route)


def from_partner(block, bits):
    n = lax.axis_size("seq")
    return lax.ppermute(block, "seq", [(i, i ^ bits) for i in range(n)])


def lag(slot, core):
    return (0, 3 - 2 * core, 2, 1 + 2 * core)[slot]


def run(body, outs, name, scalars, arrays, scratch=(), vmem=16 << 20, flops=2_000_000_000):
    many = isinstance(outs, (list, tuple))
    return pl.pallas_call(
        body,
        out_shape=outs,
        in_specs=[SM] * len(scalars) + [VM] * len(arrays),
        out_specs=[VM] * len(outs) if many else VM,
        scratch_shapes=list(scratch),
        compiler_params=pltpu.CompilerParams(vmem_limit_bytes=vmem),
        cost_estimate=pl.CostEstimate(flops=flops, transcendentals=0, bytes_accessed=flops // 200),
        name=name,
    )(*scalars, *arrays)


def dot(a, b):
    return jnp.dot(a, b, preferred_element_type=f32)


def copy_body(source, out):
    out[...] = source[...]


def merge(kept, landed, first, second):
    half = first.shape[0]
    first[...] = (kept[:half, :].astype(f32) + landed[:half, :].astype(f32)).astype(bf16)
    second[...] = (kept[half:, :].astype(f32) + landed[half:, :].astype(f32)).astype(bf16)


def norm_kv_body(place, x0, x1, x2, x3, gain, wkv, n_out, kv_out, kept):
    f, core = place[0], place[2]
    xs = (x0, x1, x2, x3)
    tokens, width = x0.shape
    step = 128
    for r in range(tokens // step):
        rows = pl.ds(r * step, step)
        total = None
        for x in xs:
            v = x[rows, :].astype(f32)
            part = jnp.sum(v * v, axis=1, keepdims=True)
            total = part if total is None else total + part
        scale = lax.rsqrt(total / (width * 4) + epsilon)
        for d, x in enumerate(xs):
            g = lax.rem(f + lag(d, core), 4)
            v = x[rows, :].astype(f32) * scale * gain[pl.ds(g, 1), :]
            n_out[d, rows, :] = v.astype(bf16)
    own = kept.shape[1]
    own_rows = pl.ds(pl.multiple_of(f * own, own), own)
    for d, x in enumerate(xs):
        kept[lax.rem(f + lag(d, core), 4)] = x[own_rows, :]
    acc = None
    for d in range(4):
        g = lax.rem(f + lag(d, core), 4)
        start = pl.multiple_of(g * width, 128)
        part = dot(n_out[d], wkv[pl.ds(start, width), :])
        acc = part if acc is None else acc + part
    kv = acc.astype(bf16)
    half = tokens // 2
    kv_out[...] = jnp.concatenate([kv[:half], kv[half:]], axis=1)


def query_body(place, n_in, wq, cosine, sine, q_out):
    f, core = place[0], place[2]
    width = n_in.shape[2]
    acc = None
    for d in range(4):
        g = lax.rem(f + lag(d, core), 4)
        start = pl.multiple_of(g * width, 128)
        part = dot(n_in[d], wq[pl.ds(start, width), :])
        acc = part if acc is None else acc + part
    factor = HD**-0.5 * math.log2(math.e)
    c = cosine[: acc.shape[0], :] * factor
    s = sine[: acc.shape[0], :] * factor
    for h in range(acc.shape[1] // HD):
        v = acc[:, h * HD : (h + 1) * HD]
        q_out[:, h * HD : (h + 1) * HD] = (v * c + pltpu.roll(v, HD // 2, 1) * s).astype(bf16)


def join_body(a, b, out):
    half = a.shape[0]
    out[:half, :] = a[...]
    out[half:, :] = b[...]


def rotate_body(place, y0, y1, y2, y3, cosine, sine, out, hold):
    f = place[0]
    for d, y in enumerate((y0, y1, y2, y3)):
        hold[lax.rem(f + d, 4)] = y[...].astype(f32)
    quarter = y0.shape[0] // 2
    for block in range(4):
        source = slice(block // 2 * quarter, block // 2 * quarter + quarter)
        lanes = slice(block % 2 * 64, block % 2 * 64 + 64)
        rows = pl.ds(block * quarter, quarter)
        k = jnp.concatenate([hold[0, source, lanes], hold[1, source, lanes]], axis=1)
        v = jnp.concatenate([hold[2, source, lanes], hold[3, source, lanes]], axis=1)
        k = k * cosine[rows, :] + pltpu.roll(k, HD // 2, 1) * sine[rows, :]
        out[rows, :HD] = k.astype(bf16)
        out[rows, HD:] = v.astype(bf16)


def attend_body(d, place, offsets, q, mine, theirs, wo, *refs):
    if d == 0:
        merge(refs[0], refs[1], refs[3], refs[4])
        refs = refs[2:3] + refs[5:]
    out, win, att = refs
    f = place[0]
    first = place[1]
    tokens = q.shape[0]
    heads = q.shape[1] // HD
    core = place[2]
    for slot, part, row in ((core, mine, 1), (1 - core, theirs, 1), (2 + core, mine, 0), (3 - core, theirs, 0)):
        rows = pl.ds(pl.multiple_of(slot * tokens, tokens), tokens)
        win[rows, :] = part[row * tokens : (row + 1) * tokens, :]
    step = 128
    b = lax.rem(f + (d if d % 2 == 0 else d + (2 - d) * 2 * core), 4)
    row0 = pl.multiple_of(b * step, step)
    key0 = pl.multiple_of(core * tokens + b * step, step)
    pos = first + row0 + lax.broadcasted_iota(jnp.int32, (step, 1), 0)
    begin = jnp.zeros((step, 1), jnp.int32)
    for r in range(offsets.shape[0]):
        begin = jnp.where(pos >= offsets[r], offsets[r], begin)
    low = jnp.maximum(pos - (WIN - 1), begin)
    low = jnp.concatenate([low] * heads, axis=0)
    high = jnp.concatenate([pos] * heads, axis=0)
    qs = jnp.concatenate([q[pl.ds(row0, step), h * HD : (h + 1) * HD] for h in range(heads)], axis=0)
    total = None
    mixed = None
    for start, size in ((0, 512), (512, 512), (1024, 128)):
        k = win[pl.ds(key0 + start, size), :HD]
        v = win[pl.ds(key0 + start, size), HD:]
        kpos = first + row0 + (start - WIN) + lax.broadcasted_iota(jnp.int32, (heads * step, size), 1)
        allowed = kpos >= low
        if start == WIN:
            allowed = allowed & (kpos <= high)
        s = lax.dot_general(qs, k, (((1,), (1,)), ((), ())), preferred_element_type=f32)
        p = jnp.where(allowed, jnp.exp2(s), 0.0)
        part = jnp.sum(p, axis=1, keepdims=True)
        total = part if total is None else total + part
        part = dot(p.astype(bf16), v)
        mixed = part if mixed is None else mixed + part
    mixed = (mixed / total).astype(bf16)
    for h in range(heads):
        att[:, h * HD : (h + 1) * HD] = mixed[h * step : (h + 1) * step]
    out[...] = dot(att[...], wo[...]).astype(out.dtype)


def residual_body(kept, p0, p1, p2, p3, gain, rows, landed, res_out, n_out, first, second):
    merge(rows, landed, first, second)
    width = kept.shape[2]
    total = None
    for g in range(4):
        cols = slice(g * width, (g + 1) * width)
        v = kept[g].astype(f32) + p0[:, cols]
        v = v + p1[:, cols].astype(f32)
        v = v + p2[:, cols].astype(f32)
        v = v + p3[:, cols].astype(f32)
        res_out[g] = v
        part = jnp.sum(v * v, axis=1, keepdims=True)
        total = part if total is None else total + part
    scale = lax.rsqrt(total / (width * 4) + epsilon)
    for g in range(4):
        cols = slice(g * width, (g + 1) * width)
        n_out[:, cols] = (res_out[g] * scale * gain[:, cols]).astype(bf16)


def gelu(x):
    inner = math.sqrt(2 / math.pi) * (x + 0.044715 * (x * x * x))
    return x * (0.5 * (1.0 + jnp.tanh(inner)))


def feed_body(count, own, before, cached, *refs):
    place = refs[0]
    blocks = refs[1 : 1 + count]
    refs = refs[1 + count :]
    if cached:
        outs, (act, hold) = refs[-2 - cached : -2], refs[-2:]
        if own:
            merge(refs[0], refs[1], *outs)
        else:
            outs[0][...] = (refs[0][...].astype(f32) + refs[1][...].astype(f32)).astype(bf16)
        refs = refs[2 : -2 - cached] + (act, hold)
    res = None
    if own:
        res, refs = refs[0], refs[1:]
    earlier = dict(zip(before, refs[: len(before)]))
    wg, wu, wd, o0, o1, o2, o3, act, hold = refs[len(before) :]
    f = place[0]
    rows, width = o0.shape
    n = jnp.concatenate([r[...] for r in blocks], axis=0) if count > 1 else blocks[0][...]
    chunk = 512
    for c in range(0, wg.shape[1], chunk):
        cols = slice(c, min(c + chunk, wg.shape[1]))
        act[:, cols] = (gelu(dot(n, wg[:, cols])) * dot(n, wu[:, cols])).astype(bf16)
    for g in (0, 2):
        pair = dot(act[...], wd[:, g * width : (g + 2) * width])
        for h in (0, 1):
            part = pair[:, h * width : (h + 1) * width]
            hold[g + h] = part + res[g + h] if own else part
    o0[...] = hold[f]
    for d, o in ((1, o1), (2, o2), (3, o3)):
        lead = o.shape[0] - rows
        if d in earlier:
            o[:lead, :] = earlier[d][...]
        target = d if d == 2 else d + (2 - d) * 2 * place[2]
        o[lead:, :] = hold[lax.rem(f + target, 4)].astype(o.dtype)


def early_sum_body(place, own, both, far, early2, early1, out):
    step = own.shape[0]
    core = place[2]
    near, other = lag(1, core), lag(3, core)
    out[0] = own[...]
    out[near] = both[:step]
    out[2] = far[...]
    out[other] = both[step:]
    for row, shift in enumerate((0, near, other)):
        rows = slice(row * step, row * step + step)
        r = lax.rem(shift + 2, 4)
        out[r] = out[r] + early2[rows].astype(f32)
        r = lax.rem(shift + near, 4)
        out[r] = out[r] + early1[rows].astype(f32)


def finish_body(place, some, late2, late1, whole, out):
    f, core = place[0], place[2]
    step = some.shape[1]
    for row, (r, more) in enumerate(((lag(3, core), late1), (0, late2), (2, None), (lag(1, core), None))):
        total = some[r] + whole[row * step : row * step + step].astype(f32)
        if more is not None:
            total = total + more[...].astype(f32)
        rows = pl.ds(pl.multiple_of(lax.rem(f + r, 4) * step, step), step)
        out[rows, :] = total.astype(bf16)


def image_body(target, other, rows, sibling, sent, kept):
    step = sent.shape[0]
    for part, out in enumerate((sent, kept)):
        index = part * step + lax.broadcasted_iota(jnp.int32, (step, target.shape[1]), 0)
        hot = jnp.where(index == target[...], 1.0, 0.0).astype(bf16)
        count = target.shape[1]
        total = dot(hot, rows[:count, :])
        hot = jnp.where(index == other[...], 1.0, 0.0).astype(bf16)
        out[...] = (total + dot(hot, sibling[:count, :])).astype(bf16)


def shards(
    hidden,
    lengths,
    page_table,
    first_gain,
    query_weight,
    keyvalue_weight,
    output_weight,
    second_gain,
    gate_weight,
    up_weight,
    down_weight,
):
    tokens, width = hidden.shape
    full = width * 4
    seq_index = lax.axis_index("seq")
    f = lax.axis_index("feat")
    first = seq_index * tokens
    place = jnp.stack([f, first, seq_index % 2]).astype(jnp.int32)
    sds = jax.ShapeDtypeStruct

    x0 = run(copy_body, sds(hidden.shape, bf16), "take_own", [], [hidden])
    x1 = to_side(hidden, (1, 3))
    x2 = from_peer(hidden, 2)
    x3 = to_side(hidden, (3, 1))

    offsets = jnp.cumsum(lengths) - lengths
    ticks = jnp.arange(tokens, dtype=jnp.int32)
    places = jnp.concatenate([first + ticks, first - WIN + ticks, (seq_index ^ 1) * tokens + ticks])
    numbers = jnp.arange(lengths.shape[0], dtype=jnp.int32)
    segment = jnp.sum((places[:, None] >= offsets[None, :]).astype(jnp.int32), axis=1) - 1
    member = (segment[:, None] == numbers[None, :]).astype(jnp.int32)
    inner = places - jnp.sum(member * offsets[None, :], axis=1)
    length = jnp.sum(member * lengths[None, :], axis=1)
    half = HD // 2
    freq = jnp.exp(jnp.arange(half, dtype=f32) * (-2.0 * math.log(10000.0) / HD))
    angle = inner[: 2 * tokens].astype(f32)[:, None] * freq[None, :]
    cosine = jnp.cos(angle)
    sine = jnp.sin(angle)
    cosine = jnp.concatenate([cosine, cosine], axis=1)
    sine = jnp.concatenate([-sine, sine], axis=1)

    pages = page_table.shape[0]
    part_rows = BLK // 4
    keep = inner >= length - WIN
    slot = inner % WIN
    entry = segment * (WIN // BLK) + slot // BLK
    page = jnp.sum(
        jnp.where(
            entry[:, None] == jnp.arange(pages, dtype=jnp.int32)[None, :], page_table[None, :], 0
        ),
        axis=1,
    )
    within = slot % BLK
    owner = page // 2

    def rank(mine, theirs):
        apart = mine ^ theirs
        return jnp.where(apart == 1, 0, jnp.where(apart == 2, 1, jnp.where(apart == 0, 2, 3)))

    column = rank(seq_index // 8, owner // 8) * 4 + rank(seq_index // 2 % 4, owner // 2 % 4)
    mine = keep & (within // part_rows == f) & (owner % 2 == seq_index % 2)
    target = jnp.where(mine, (column * 2 + page % 2) * part_rows + within % part_rows, -1)
    other = target[None, 2 * tokens :]
    target = target[None, :tokens]
    held_rows = 2 * part_rows

    gain1 = first_gain.reshape(4, width)
    gain2 = second_gain.reshape(1, full)
    x1, x2, x3, target, other, cosine, sine, offsets, place, gain1, gain2 = lax.optimization_barrier(
        (x1, x2, x3, target, other, cosine, sine, offsets, place, gain1, gain2)
    )
    step = tokens // 4

    normed, kv_part, kept = run(
        norm_kv_body,
        (
            sds((4, tokens, width), bf16),
            sds((tokens // 2, 128), bf16),
            sds((4, step, width), bf16),
        ),
        "norm_kv",
        [place],
        [x0, x1, x2, x3, gain1, keyvalue_weight],
    )
    far_part = from_earlier(kv_part, 2)
    queries = run(
        query_body,
        sds((tokens, query_weight.shape[1]), bf16),
        "queries",
        [place],
        [normed, query_weight, cosine, sine],
    )
    far_part, queries = lax.optimization_barrier((far_part, queries))
    y0 = run(join_body, sds((tokens, 128), bf16), "join", [], [kv_part, far_part])
    y2, y1, y3 = from_peer(y0, 2), from_peer(y0, 1), from_peer(y0, 3)
    mine = run(
        rotate_body,
        sds((2 * tokens, 2 * HD), bf16),
        "rotate",
        [place],
        [y0, y1, y2, y3, cosine, sine],
        [pltpu.VMEM((4, tokens, 128), f32)],
    )
    theirs = from_partner(mine, 1)
    def halves(rows):
        return [sds((rows.shape[0] // 2, 2 * HD), bf16)] * 2

    def attend(d, kind, cached=()):
        out = sds((step, full), kind)
        return run(
            functools.partial(attend_body, d),
            [out, *halves(cached[0])] if cached else out,
            f"attend{d}",
            [place, offsets],
            [queries, mine, theirs, output_weight, *cached],
            [
                pltpu.VMEM((4 * tokens, 2 * HD), bf16),
                pltpu.VMEM((step, query_weight.shape[1]), bf16),
            ],
        )

    s2 = attend(2, bf16)
    p2 = from_peer(s2, 2)
    image_sent, image_kept = run(
        image_body,
        [sds((8 * held_rows, 2 * HD), bf16)] * 2,
        "image",
        [],
        [target, other, mine, theirs],
    )
    landed = from_partner(image_sent, 8)

    p1 = to_side(attend(1, bf16), (1, 3))
    p3 = to_side(attend(3, bf16), (3, 1))
    p0, stay, go = attend(0, f32, [image_kept, landed])
    landed = from_partner(go, 24)
    residual, normed2, go, stay = run(
        residual_body,
        [sds((4, step, width), f32), sds((step, full), bf16), *halves(stay)],
        "residual",
        [],
        [kept, p0, p1, p2, p3, gain2, stay, landed],
    )
    landed = from_partner(go, 2)
    m1 = to_side(normed2, (1, 3))
    m3 = to_side(normed2, (3, 1))
    hidden_units = gate_weight.shape[1]

    def feed(name, blocks, res=(), before=(), cached=()):
        rows = sum(block.shape[0] for block in blocks)
        lead = {d: rows_before.shape[0] for d, rows_before in before}
        outs = [sds((rows, width), f32)]
        outs += [sds((rows + lead.get(d, 0), width), bf16) for d in (1, 2, 3)]
        more = []
        if cached:
            more = halves(cached[0]) if res else [sds(cached[0].shape, bf16)]
        return run(
            functools.partial(feed_body, len(blocks), bool(res), tuple(lead), len(more)),
            outs + more,
            name,
            [place],
            [*blocks, *cached, *res, *(b for _, b in before), gate_weight, up_weight, down_weight],
            [pltpu.VMEM((rows, hidden_units), bf16), pltpu.VMEM((4, rows, width), f32)],
            vmem=24 << 20,
            flops=20_000_000_000 if before and cached else 2_000_000_000,
        )

    own0, *own_sent, stay, go = feed("feed_own", [normed2], res=[residual], cached=[stay, landed])
    landed = from_partner(go, 6)
    m1, _ = lax.optimization_barrier((m1, own0))
    m2 = to_side(m1, (1, 3))
    both0, early1, early2, early3, cache = feed(
        "feed_near", [m1, m3], before=list(zip((1, 2, 3), own_sent)), cached=[stay, landed]
    )
    early2 = from_peer(early2, 2)
    early1 = to_side(early1, (1, 3))
    far0, late1, late2, whole = feed("feed_far", [m2], before=[(3, early3)])
    whole = to_side(whole, (3, 1))
    late2 = from_peer(late2, 2)
    late1 = to_side(late1, (1, 3))
    some = run(
        early_sum_body,
        sds((4, step, width), f32),
        "early_sum",
        [place],
        [own0, both0, far0, early2, early1],
        flops=10_000_000_000,
    )
    output = run(
        finish_body,
        sds((tokens, width), bf16),
        "finish",
        [place],
        [some, late2, late1, whole],
    )
    return (output, cache.reshape(2, part_rows, 2 * HD))


def solution(mesh):
    placed = (
        P("seq", "feat"),
        P(),
        P(),
        P(),
        P(None, "feat"),
        P(None, "feat"),
        P("feat", None),
        P(),
        P(None, "feat"),
        P(None, "feat"),
        P("feat", None),
    )
    return jax.shard_map(
        shards,
        mesh=mesh,
        in_specs=placed,
        out_specs=(P("seq", "feat"), P("seq", "feat", None)),
        check_vma=False,
    )
```

```python
import functools
import math

import jax
import jax.numpy as jnp
from jax import lax
from jax.experimental import pallas as pl
from jax.experimental.pallas import tpu as pltpu
from jax.sharding import PartitionSpec as P

HD = 128
WIN = 1024
BLK = 128
epsilon = 1e-06
bf16 = jnp.bfloat16
f32 = jnp.float32
VM = pl.BlockSpec(memory_space=pltpu.VMEM)
SM = pl.BlockSpec(memory_space=pltpu.SMEM)


def from_peer(block, distance):
    n = lax.axis_size("feat")
    return lax.ppermute(block, "feat", [(i, (i - distance) % n) for i in range(n)])


def from_earlier(block, distance):
    n = lax.axis_size("seq")
    return lax.ppermute(block, "seq", [(i - distance, i) for i in range(distance, n)])


def to_side(block, distances):
    n, m = lax.axis_size("seq"), lax.axis_size("feat")
    route = [(i * m + j, i * m + (j + distances[i % 2]) % m) for i in range(n) for j in range(m)]
    return lax.ppermute(block, ("seq", "feat"), route)


def from_partner(block, bits):
    n = lax.axis_size("seq")
    return lax.ppermute(block, "seq", [(i, i ^ bits) for i in range(n)])


def lag(slot, core):
    return (0, 3 - 2 * core, 2, 1 + 2 * core)[slot]


def run(body, outs, name, scalars, arrays, scratch=(), vmem=16 << 20, flops=2_000_000_000):
    many = isinstance(outs, (list, tuple))
    return pl.pallas_call(
        body,
        out_shape=outs,
        in_specs=[SM] * len(scalars) + [VM] * len(arrays),
        out_specs=[VM] * len(outs) if many else VM,
        scratch_shapes=list(scratch),
        compiler_params=pltpu.CompilerParams(vmem_limit_bytes=vmem),
        cost_estimate=pl.CostEstimate(flops=flops, transcendentals=0, bytes_accessed=flops // 200),
        name=name,
    )(*scalars, *arrays)


def dot(a, b):
    return jnp.dot(a, b, preferred_element_type=f32)


def copy_body(source, out):
    out[...] = source[...]


def merge(kept, landed, first, second):
    half = first.shape[0]
    first[...] = (kept[:half, :].astype(f32) + landed[:half, :].astype(f32)).astype(bf16)
    second[...] = (kept[half:, :].astype(f32) + landed[half:, :].astype(f32)).astype(bf16)


def norm_kv_body(place, x0, x1, x2, x3, gain, wkv, n_out, kv_out, kept):
    f, core = place[0], place[2]
    xs = (x0, x1, x2, x3)
    tokens, width = x0.shape
    step = 128
    for r in range(tokens // step):
        rows = pl.ds(r * step, step)
        total = None
        for x in xs:
            v = x[rows, :].astype(f32)
            part = jnp.sum(v * v, axis=1, keepdims=True)
            total = part if total is None else total + part
        scale = lax.rsqrt(total / (width * 4) + epsilon)
        for d, x in enumerate(xs):
            g = lax.rem(f + lag(d, core), 4)
            v = x[rows, :].astype(f32) * scale * gain[pl.ds(g, 1), :]
            n_out[d, rows, :] = v.astype(bf16)
    own = kept.shape[1]
    own_rows = pl.ds(pl.multiple_of(f * own, own), own)
    for d, x in enumerate(xs):
        kept[lax.rem(f + lag(d, core), 4)] = x[own_rows, :]
    acc = None
    for d in range(4):
        g = lax.rem(f + lag(d, core), 4)
        start = pl.multiple_of(g * width, 128)
        part = dot(n_out[d], wkv[pl.ds(start, width), :])
        acc = part if acc is None else acc + part
    kv = acc.astype(bf16)
    half = tokens // 2
    kv_out[...] = jnp.concatenate([kv[:half], kv[half:]], axis=1)


def query_body(place, n_in, wq, cosine, sine, q_out):
    f, core = place[0], place[2]
    width = n_in.shape[2]
    acc = None
    for d in range(4):
        g = lax.rem(f + lag(d, core), 4)
        start = pl.multiple_of(g * width, 128)
        part = dot(n_in[d], wq[pl.ds(start, width), :])
        acc = part if acc is None else acc + part
    factor = HD**-0.5 * math.log2(math.e)
    c = cosine[: acc.shape[0], :] * factor
    s = sine[: acc.shape[0], :] * factor
    for h in range(acc.shape[1] // HD):
        v = acc[:, h * HD : (h + 1) * HD]
        q_out[:, h * HD : (h + 1) * HD] = (v * c + pltpu.roll(v, HD // 2, 1) * s).astype(bf16)


def join_body(a, b, out):
    half = a.shape[0]
    out[:half, :] = a[...]
    out[half:, :] = b[...]


def rotate_body(place, y0, y1, y2, y3, cosine, sine, out, hold):
    f = place[0]
    for d, y in enumerate((y0, y1, y2, y3)):
        hold[lax.rem(f + d, 4)] = y[...].astype(f32)
    quarter = y0.shape[0] // 2
    for block in range(4):
        source = slice(block // 2 * quarter, block // 2 * quarter + quarter)
        lanes = slice(block % 2 * 64, block % 2 * 64 + 64)
        rows = pl.ds(block * quarter, quarter)
        k = jnp.concatenate([hold[0, source, lanes], hold[1, source, lanes]], axis=1)
        v = jnp.concatenate([hold[2, source, lanes], hold[3, source, lanes]], axis=1)
        k = k * cosine[rows, :] + pltpu.roll(k, HD // 2, 1) * sine[rows, :]
        out[rows, :HD] = k.astype(bf16)
        out[rows, HD:] = v.astype(bf16)


def attend_body(d, place, offsets, q, mine, theirs, wo, *refs):
    if d == 0:
        merge(refs[0], refs[1], refs[3], refs[4])
        refs = refs[2:3] + refs[5:]
    out, win, att = refs
    f = place[0]
    first = place[1]
    tokens = q.shape[0]
    heads = q.shape[1] // HD
    core = place[2]
    for slot, part, row in ((core, mine, 1), (1 - core, theirs, 1), (2 + core, mine, 0), (3 - core, theirs, 0)):
        rows = pl.ds(pl.multiple_of(slot * tokens, tokens), tokens)
        win[rows, :] = part[row * tokens : (row + 1) * tokens, :]
    step = 128
    b = lax.rem(f + (d if d % 2 == 0 else d + (2 - d) * 2 * core), 4)
    row0 = pl.multiple_of(b * step, step)
    key0 = pl.multiple_of(core * tokens + b * step, step)
    pos = first + row0 + lax.broadcasted_iota(jnp.int32, (step, 1), 0)
    begin = jnp.zeros((step, 1), jnp.int32)
    for r in range(offsets.shape[0]):
        begin = jnp.where(pos >= offsets[r], offsets[r], begin)
    low = jnp.maximum(pos - (WIN - 1), begin)
    low = jnp.concatenate([low] * heads, axis=0)
    high = jnp.concatenate([pos] * heads, axis=0)
    qs = jnp.concatenate([q[pl.ds(row0, step), h * HD : (h + 1) * HD] for h in range(heads)], axis=0)
    total = None
    mixed = None
    for start, size in ((0, 512), (512, 512), (1024, 128)):
        k = win[pl.ds(key0 + start, size), :HD]
        v = win[pl.ds(key0 + start, size), HD:]
        kpos = first + row0 + (start - WIN) + lax.broadcasted_iota(jnp.int32, (heads * step, size), 1)
        allowed = kpos >= low
        if start == WIN:
            allowed = allowed & (kpos <= high)
        s = lax.dot_general(qs, k, (((1,), (1,)), ((), ())), preferred_element_type=f32)
        p = jnp.where(allowed, jnp.exp2(s), 0.0)
        part = jnp.sum(p, axis=1, keepdims=True)
        total = part if total is None else total + part
        part = dot(p.astype(bf16), v)
        mixed = part if mixed is None else mixed + part
    mixed = (mixed / total).astype(bf16)
    for h in range(heads):
        att[:, h * HD : (h + 1) * HD] = mixed[h * step : (h + 1) * step]
    out[...] = dot(att[...], wo[...]).astype(out.dtype)


def residual_body(kept, p0, p1, p2, p3, gain, rows, landed, res_out, n_out, first, second):
    merge(rows, landed, first, second)
    width = kept.shape[2]
    total = None
    for g in range(4):
        cols = slice(g * width, (g + 1) * width)
        v = kept[g].astype(f32) + p0[:, cols]
        v = v + p1[:, cols].astype(f32)
        v = v + p2[:, cols].astype(f32)
        v = v + p3[:, cols].astype(f32)
        res_out[g] = v
        part = jnp.sum(v * v, axis=1, keepdims=True)
        total = part if total is None else total + part
    scale = lax.rsqrt(total / (width * 4) + epsilon)
    for g in range(4):
        cols = slice(g * width, (g + 1) * width)
        n_out[:, cols] = (res_out[g] * scale * gain[:, cols]).astype(bf16)


def gelu(x):
    inner = math.sqrt(2 / math.pi) * (x + 0.044715 * (x * x * x))
    return x * (0.5 * (1.0 + jnp.tanh(inner)))


def feed_body(count, own, before, cached, *refs):
    place = refs[0]
    blocks = refs[1 : 1 + count]
    refs = refs[1 + count :]
    if cached:
        outs, (act, hold) = refs[-2 - cached : -2], refs[-2:]
        if own:
            merge(refs[0], refs[1], *outs)
        else:
            outs[0][...] = (refs[0][...].astype(f32) + refs[1][...].astype(f32)).astype(bf16)
        refs = refs[2 : -2 - cached] + (act, hold)
    res = None
    if own:
        res, refs = refs[0], refs[1:]
    earlier = dict(zip(before, refs[: len(before)]))
    wg, wu, wd, o0, o1, o2, o3, act, hold = refs[len(before) :]
    f = place[0]
    rows, width = o0.shape
    n = jnp.concatenate([r[...] for r in blocks], axis=0) if count > 1 else blocks[0][...]
    chunk = 512
    for c in range(0, wg.shape[1], chunk):
        cols = slice(c, min(c + chunk, wg.shape[1]))
        act[:, cols] = (gelu(dot(n, wg[:, cols])) * dot(n, wu[:, cols])).astype(bf16)
    for g in (0, 2):
        pair = dot(act[...], wd[:, g * width : (g + 2) * width])
        for h in (0, 1):
            part = pair[:, h * width : (h + 1) * width]
            hold[g + h] = part + res[g + h] if own else part
    o0[...] = hold[f]
    for d, o in ((1, o1), (2, o2), (3, o3)):
        lead = o.shape[0] - rows
        if d in earlier:
            o[:lead, :] = earlier[d][...]
        target = d if d == 2 else d + (2 - d) * 2 * place[2]
        o[lead:, :] = hold[lax.rem(f + target, 4)].astype(o.dtype)


def early_sum_body(place, own, both, far, early2, early1, stay, landed, out, cache):
    step = own.shape[0]
    cache[...] = (stay[...].astype(f32) + landed[...].astype(f32)).astype(bf16)
    core = place[2]
    near, other = lag(1, core), lag(3, core)
    out[0] = own[...]
    out[near] = both[:step]
    out[2] = far[...]
    out[other] = both[step:]
    for row, shift in enumerate((0, near, other)):
        rows = slice(row * step, row * step + step)
        r = lax.rem(shift + 2, 4)
        out[r] = out[r] + early2[rows].astype(f32)
        r = lax.rem(shift + near, 4)
        out[r] = out[r] + early1[rows].astype(f32)


def finish_body(place, some, late2, late1, whole, out):
    f, core = place[0], place[2]
    step = some.shape[1]
    for row, (r, more) in enumerate(((lag(3, core), late1), (0, late2), (2, None), (lag(1, core), None))):
        total = some[r] + whole[row * step : row * step + step].astype(f32)
        if more is not None:
            total = total + more[...].astype(f32)
        rows = pl.ds(pl.multiple_of(lax.rem(f + r, 4) * step, step), step)
        out[rows, :] = total.astype(bf16)


def image_body(target, other, rows, sibling, sent, kept):
    step = sent.shape[0]
    for part, out in enumerate((sent, kept)):
        index = part * step + lax.broadcasted_iota(jnp.int32, (step, target.shape[1]), 0)
        hot = jnp.where(index == target[...], 1.0, 0.0).astype(bf16)
        count = target.shape[1]
        total = dot(hot, rows[:count, :])
        hot = jnp.where(index == other[...], 1.0, 0.0).astype(bf16)
        out[...] = (total + dot(hot, sibling[:count, :])).astype(bf16)


def shards(
    hidden,
    lengths,
    page_table,
    first_gain,
    query_weight,
    keyvalue_weight,
    output_weight,
    second_gain,
    gate_weight,
    up_weight,
    down_weight,
):
    tokens, width = hidden.shape
    full = width * 4
    seq_index = lax.axis_index("seq")
    f = lax.axis_index("feat")
    first = seq_index * tokens
    place = jnp.stack([f, first, seq_index % 2]).astype(jnp.int32)
    sds = jax.ShapeDtypeStruct

    x0 = run(copy_body, sds(hidden.shape, bf16), "take_own", [], [hidden])
    x1 = to_side(hidden, (1, 3))
    x2 = from_peer(hidden, 2)
    x3 = to_side(hidden, (3, 1))

    offsets = jnp.cumsum(lengths) - lengths
    ticks = jnp.arange(tokens, dtype=jnp.int32)
    places = jnp.concatenate([first + ticks, first - WIN + ticks, (seq_index ^ 1) * tokens + ticks])
    numbers = jnp.arange(lengths.shape[0], dtype=jnp.int32)
    segment = jnp.sum((places[:, None] >= offsets[None, :]).astype(jnp.int32), axis=1) - 1
    member = (segment[:, None] == numbers[None, :]).astype(jnp.int32)
    inner = places - jnp.sum(member * offsets[None, :], axis=1)
    length = jnp.sum(member * lengths[None, :], axis=1)
    half = HD // 2
    freq = jnp.exp(jnp.arange(half, dtype=f32) * (-2.0 * math.log(10000.0) / HD))
    angle = inner[: 2 * tokens].astype(f32)[:, None] * freq[None, :]
    cosine = jnp.cos(angle)
    sine = jnp.sin(angle)
    cosine = jnp.concatenate([cosine, cosine], axis=1)
    sine = jnp.concatenate([-sine, sine], axis=1)

    pages = page_table.shape[0]
    part_rows = BLK // 4
    keep = inner >= length - WIN
    slot = inner % WIN
    entry = segment * (WIN // BLK) + slot // BLK
    page = jnp.sum(
        jnp.where(
            entry[:, None] == jnp.arange(pages, dtype=jnp.int32)[None, :], page_table[None, :], 0
        ),
        axis=1,
    )
    within = slot % BLK
    owner = page // 2

    def rank(mine, theirs):
        apart = mine ^ theirs
        return jnp.where(apart == 1, 0, jnp.where(apart == 2, 1, jnp.where(apart == 0, 2, 3)))

    column = rank(seq_index // 8, owner // 8) * 4 + rank(seq_index // 2 % 4, owner // 2 % 4)
    mine = keep & (within // part_rows == f) & (owner % 2 == seq_index % 2)
    target = jnp.where(mine, (column * 2 + page % 2) * part_rows + within % part_rows, -1)
    other = target[None, 2 * tokens :]
    target = target[None, :tokens]
    held_rows = 2 * part_rows

    gain1 = first_gain.reshape(4, width)
    gain2 = second_gain.reshape(1, full)
    x1, x2, x3, target, other, cosine, sine, offsets, place, gain1, gain2 = lax.optimization_barrier(
        (x1, x2, x3, target, other, cosine, sine, offsets, place, gain1, gain2)
    )
    step = tokens // 4

    normed, kv_part, kept = run(
        norm_kv_body,
        (
            sds((4, tokens, width), bf16),
            sds((tokens // 2, 128), bf16),
            sds((4, step, width), bf16),
        ),
        "norm_kv",
        [place],
        [x0, x1, x2, x3, gain1, keyvalue_weight],
    )
    far_part = from_earlier(kv_part, 2)
    queries = run(
        query_body,
        sds((tokens, query_weight.shape[1]), bf16),
        "queries",
        [place],
        [normed, query_weight, cosine, sine],
    )
    far_part, queries = lax.optimization_barrier((far_part, queries))
    y0 = run(join_body, sds((tokens, 128), bf16), "join", [], [kv_part, far_part])
    y2, y1, y3 = from_peer(y0, 2), from_peer(y0, 1), from_peer(y0, 3)
    mine = run(
        rotate_body,
        sds((2 * tokens, 2 * HD), bf16),
        "rotate",
        [place],
        [y0, y1, y2, y3, cosine, sine],
        [pltpu.VMEM((4, tokens, 128), f32)],
    )
    theirs = from_partner(mine, 1)
    def halves(rows):
        return [sds((rows.shape[0] // 2, 2 * HD), bf16)] * 2

    def attend(d, kind, cached=()):
        out = sds((step, full), kind)
        return run(
            functools.partial(attend_body, d),
            [out, *halves(cached[0])] if cached else out,
            f"attend{d}",
            [place, offsets],
            [queries, mine, theirs, output_weight, *cached],
            [
                pltpu.VMEM((4 * tokens, 2 * HD), bf16),
                pltpu.VMEM((step, query_weight.shape[1]), bf16),
            ],
        )

    s2 = attend(2, bf16)
    p2 = from_peer(s2, 2)
    image_sent, image_kept = run(
        image_body,
        [sds((8 * held_rows, 2 * HD), bf16)] * 2,
        "image",
        [],
        [target, other, mine, theirs],
    )
    landed = from_partner(image_sent, 8)

    p1 = to_side(attend(1, bf16), (1, 3))
    p3 = to_side(attend(3, bf16), (3, 1))
    p0, stay, go = attend(0, f32, [image_kept, landed])
    landed = from_partner(go, 24)
    residual, normed2, go, stay = run(
        residual_body,
        [sds((4, step, width), f32), sds((step, full), bf16), *halves(stay)],
        "residual",
        [],
        [kept, p0, p1, p2, p3, gain2, stay, landed],
    )
    landed = from_partner(go, 2)
    m1 = to_side(normed2, (1, 3))
    m3 = to_side(normed2, (3, 1))
    hidden_units = gate_weight.shape[1]

    def feed(name, blocks, res=(), before=(), cached=()):
        rows = sum(block.shape[0] for block in blocks)
        lead = {d: rows_before.shape[0] for d, rows_before in before}
        outs = [sds((rows, width), f32)]
        outs += [sds((rows + lead.get(d, 0), width), bf16) for d in (1, 2, 3)]
        more = []
        if cached:
            more = halves(cached[0]) if res else [sds(cached[0].shape, bf16)]
        return run(
            functools.partial(feed_body, len(blocks), bool(res), tuple(lead), len(more)),
            outs + more,
            name,
            [place],
            [*blocks, *cached, *res, *(b for _, b in before), gate_weight, up_weight, down_weight],
            [pltpu.VMEM((rows, hidden_units), bf16), pltpu.VMEM((4, rows, width), f32)],
            vmem=24 << 20,
            flops=20_000_000_000 if len(before) == 3 else 2_000_000_000,
        )

    own0, *own_sent, stay, go = feed("feed_own", [normed2], res=[residual], cached=[stay, landed])
    landed = from_partner(go, 6)
    m1, _ = lax.optimization_barrier((m1, own0))
    m2 = to_side(m1, (1, 3))
    both0, early1, early2, early3 = feed(
        "feed_near", [m1, m3], before=list(zip((1, 2, 3), own_sent))
    )
    early2 = from_peer(early2, 2)
    early1 = to_side(early1, (1, 3))
    far0, late1, late2, whole = feed("feed_far", [m2], before=[(3, early3)])
    whole = to_side(whole, (3, 1))
    late2 = from_peer(late2, 2)
    late1 = to_side(late1, (1, 3))
    some, cache = run(
        early_sum_body,
        [sds((4, step, width), f32), sds((held_rows, 2 * HD), bf16)],
        "early_sum",
        [place],
        [own0, both0, far0, early2, early1, stay, landed],
        flops=10_000_000_000,
    )
    output = run(
        finish_body,
        sds((tokens, width), bf16),
        "finish",
        [place],
        [some, late2, late1, whole],
    )
    return (output, cache.reshape(2, part_rows, 2 * HD))


def solution(mesh):
    placed = (
        P("seq", "feat"),
        P(),
        P(),
        P(),
        P(None, "feat"),
        P(None, "feat"),
        P("feat", None),
        P(),
        P(None, "feat"),
        P(None, "feat"),
        P("feat", None),
    )
    return jax.shard_map(
        shards,
        mesh=mesh,
        in_specs=placed,
        out_specs=(P("seq", "feat"), P("seq", "feat", None)),
        check_vma=False,
    )
```

```python
import functools
import math

import jax
import jax.numpy as jnp
from jax import lax
from jax.experimental import pallas as pl
from jax.experimental.pallas import tpu as pltpu
from jax.sharding import PartitionSpec as P

HD = 128
WIN = 1024
BLK = 128
epsilon = 1e-06
bf16 = jnp.bfloat16
f32 = jnp.float32
VM = pl.BlockSpec(memory_space=pltpu.VMEM)
SM = pl.BlockSpec(memory_space=pltpu.SMEM)


def from_peer(block, distance):
    n = lax.axis_size("feat")
    return lax.ppermute(block, "feat", [(i, (i - distance) % n) for i in range(n)])


def from_earlier(block, distance):
    n = lax.axis_size("seq")
    return lax.ppermute(block, "seq", [(i - distance, i) for i in range(distance, n)])


def to_side(block, distances):
    n, m = lax.axis_size("seq"), lax.axis_size("feat")
    route = [(i * m + j, i * m + (j + distances[i % 2]) % m) for i in range(n) for j in range(m)]
    return lax.ppermute(block, ("seq", "feat"), route)


def from_partner(block, bits):
    n = lax.axis_size("seq")
    return lax.ppermute(block, "seq", [(i, i ^ bits) for i in range(n)])


def lag(slot, core):
    return (0, 3 - 2 * core, 2, 1 + 2 * core)[slot]


def run(body, outs, name, scalars, arrays, scratch=(), vmem=16 << 20, flops=2_000_000_000):
    many = isinstance(outs, (list, tuple))
    return pl.pallas_call(
        body,
        out_shape=outs,
        in_specs=[SM] * len(scalars) + [VM] * len(arrays),
        out_specs=[VM] * len(outs) if many else VM,
        scratch_shapes=list(scratch),
        compiler_params=pltpu.CompilerParams(vmem_limit_bytes=vmem),
        cost_estimate=pl.CostEstimate(flops=flops, transcendentals=0, bytes_accessed=flops // 200),
        name=name,
    )(*scalars, *arrays)


def dot(a, b):
    return jnp.dot(a, b, preferred_element_type=f32)


def copy_body(source, out):
    out[...] = source[...]


def merge(kept, landed, first, second):
    half = first.shape[0]
    first[...] = (kept[:half, :].astype(f32) + landed[:half, :].astype(f32)).astype(bf16)
    second[...] = (kept[half:, :].astype(f32) + landed[half:, :].astype(f32)).astype(bf16)


def norm_kv_body(place, x0, x1, x2, x3, gain, wkv, n_out, kv_out, kept):
    f, core = place[0], place[2]
    xs = (x0, x1, x2, x3)
    tokens, width = x0.shape
    step = 128
    for r in range(tokens // step):
        rows = pl.ds(r * step, step)
        total = None
        for x in xs:
            v = x[rows, :].astype(f32)
            part = jnp.sum(v * v, axis=1, keepdims=True)
            total = part if total is None else total + part
        scale = lax.rsqrt(total / (width * 4) + epsilon)
        for d, x in enumerate(xs):
            g = lax.rem(f + lag(d, core), 4)
            v = x[rows, :].astype(f32) * scale * gain[pl.ds(g, 1), :]
            n_out[d, rows, :] = v.astype(bf16)
    own = kept.shape[1]
    own_rows = pl.ds(pl.multiple_of(f * own, own), own)
    for d, x in enumerate(xs):
        kept[lax.rem(f + lag(d, core), 4)] = x[own_rows, :]
    acc = None
    for d in range(4):
        g = lax.rem(f + lag(d, core), 4)
        start = pl.multiple_of(g * width, 128)
        part = dot(n_out[d], wkv[pl.ds(start, width), :])
        acc = part if acc is None else acc + part
    kv = acc.astype(bf16)
    half = tokens // 2
    kv_out[...] = jnp.concatenate([kv[:half], kv[half:]], axis=1)


def query_body(place, n_in, wq, cosine, sine, q_out):
    f, core = place[0], place[2]
    width = n_in.shape[2]
    acc = None
    for d in range(4):
        g = lax.rem(f + lag(d, core), 4)
        start = pl.multiple_of(g * width, 128)
        part = dot(n_in[d], wq[pl.ds(start, width), :])
        acc = part if acc is None else acc + part
    factor = HD**-0.5 * math.log2(math.e)
    c = cosine[: acc.shape[0], :] * factor
    s = sine[: acc.shape[0], :] * factor
    for h in range(acc.shape[1] // HD):
        v = acc[:, h * HD : (h + 1) * HD]
        q_out[:, h * HD : (h + 1) * HD] = (v * c + pltpu.roll(v, HD // 2, 1) * s).astype(bf16)


def join_body(a, b, out):
    half = a.shape[0]
    out[:half, :] = a[...]
    out[half:, :] = b[...]


def rotate_body(place, y0, y1, y2, y3, cosine, sine, out, hold):
    f = place[0]
    for d, y in enumerate((y0, y1, y2, y3)):
        hold[lax.rem(f + d, 4)] = y[...].astype(f32)
    quarter = y0.shape[0] // 2
    for block in range(4):
        source = slice(block // 2 * quarter, block // 2 * quarter + quarter)
        lanes = slice(block % 2 * 64, block % 2 * 64 + 64)
        rows = pl.ds(block * quarter, quarter)
        k = jnp.concatenate([hold[0, source, lanes], hold[1, source, lanes]], axis=1)
        v = jnp.concatenate([hold[2, source, lanes], hold[3, source, lanes]], axis=1)
        k = k * cosine[rows, :] + pltpu.roll(k, HD // 2, 1) * sine[rows, :]
        out[rows, :HD] = k.astype(bf16)
        out[rows, HD:] = v.astype(bf16)


def attend_body(d, place, offsets, q, mine, theirs, wo, *refs):
    if d == 0:
        merge(refs[0], refs[1], refs[3], refs[4])
        refs = refs[2:3] + refs[5:]
    out, win, att = refs
    f = place[0]
    first = place[1]
    tokens = q.shape[0]
    heads = q.shape[1] // HD
    core = place[2]
    for slot, part, row in ((core, mine, 1), (1 - core, theirs, 1), (2 + core, mine, 0), (3 - core, theirs, 0)):
        rows = pl.ds(pl.multiple_of(slot * tokens, tokens), tokens)
        win[rows, :] = part[row * tokens : (row + 1) * tokens, :]
    step = 128
    b = lax.rem(f + (d if d % 2 == 0 else d + (2 - d) * 2 * core), 4)
    row0 = pl.multiple_of(b * step, step)
    key0 = pl.multiple_of(core * tokens + b * step, step)
    pos = first + row0 + lax.broadcasted_iota(jnp.int32, (step, 1), 0)
    begin = jnp.zeros((step, 1), jnp.int32)
    for r in range(offsets.shape[0]):
        begin = jnp.where(pos >= offsets[r], offsets[r], begin)
    low = jnp.maximum(pos - (WIN - 1), begin)
    low = jnp.concatenate([low] * heads, axis=0)
    high = jnp.concatenate([pos] * heads, axis=0)
    qs = jnp.concatenate([q[pl.ds(row0, step), h * HD : (h + 1) * HD] for h in range(heads)], axis=0)
    total = None
    mixed = None
    for start, size in ((0, 512), (512, 512), (1024, 128)):
        k = win[pl.ds(key0 + start, size), :HD]
        v = win[pl.ds(key0 + start, size), HD:]
        kpos = first + row0 + (start - WIN) + lax.broadcasted_iota(jnp.int32, (heads * step, size), 1)
        allowed = kpos >= low
        if start == WIN:
            allowed = allowed & (kpos <= high)
        s = lax.dot_general(qs, k, (((1,), (1,)), ((), ())), preferred_element_type=f32)
        p = jnp.where(allowed, jnp.exp2(s), 0.0)
        part = jnp.sum(p, axis=1, keepdims=True)
        total = part if total is None else total + part
        part = dot(p.astype(bf16), v)
        mixed = part if mixed is None else mixed + part
    mixed = (mixed / total).astype(bf16)
    for h in range(heads):
        att[:, h * HD : (h + 1) * HD] = mixed[h * step : (h + 1) * step]
    out[...] = dot(att[...], wo[...]).astype(out.dtype)


def residual_body(kept, p0, p1, p2, p3, gain, rows, landed, res_out, n_out, first, second):
    merge(rows, landed, first, second)
    width = kept.shape[2]
    total = None
    for g in range(4):
        cols = slice(g * width, (g + 1) * width)
        v = kept[g].astype(f32) + p0[:, cols]
        v = v + p1[:, cols].astype(f32)
        v = v + p2[:, cols].astype(f32)
        v = v + p3[:, cols].astype(f32)
        res_out[g] = v
        part = jnp.sum(v * v, axis=1, keepdims=True)
        total = part if total is None else total + part
    scale = lax.rsqrt(total / (width * 4) + epsilon)
    for g in range(4):
        cols = slice(g * width, (g + 1) * width)
        n_out[:, cols] = (res_out[g] * scale * gain[:, cols]).astype(bf16)


def gelu(x):
    inner = math.sqrt(2 / math.pi) * (x + 0.044715 * (x * x * x))
    return x * (0.5 * (1.0 + jnp.tanh(inner)))


def feed_body(count, own, before, cached, *refs):
    place = refs[0]
    blocks = refs[1 : 1 + count]
    refs = refs[1 + count :]
    if cached:
        outs, (act, hold) = refs[-2 - cached : -2], refs[-2:]
        if own:
            merge(refs[0], refs[1], *outs)
        else:
            outs[0][...] = (refs[0][...].astype(f32) + refs[1][...].astype(f32)).astype(bf16)
        refs = refs[2 : -2 - cached] + (act, hold)
    res = None
    if own:
        res, refs = refs[0], refs[1:]
    earlier = dict(zip(before, refs[: len(before)]))
    wg, wu, wd, o0, o1, o2, o3, act, hold = refs[len(before) :]
    f = place[0]
    rows, width = o0.shape
    n = jnp.concatenate([r[...] for r in blocks], axis=0) if count > 1 else blocks[0][...]
    chunk = 512
    for c in range(0, wg.shape[1], chunk):
        cols = slice(c, min(c + chunk, wg.shape[1]))
        act[:, cols] = (gelu(dot(n, wg[:, cols])) * dot(n, wu[:, cols])).astype(bf16)
    for g in (0, 2):
        pair = dot(act[...], wd[:, g * width : (g + 2) * width])
        for h in (0, 1):
            part = pair[:, h * width : (h + 1) * width]
            hold[g + h] = part + res[g + h] if own else part
    o0[...] = hold[f]
    for d, o in ((1, o1), (2, o2), (3, o3)):
        lead = o.shape[0] - rows
        if d in earlier:
            o[:lead, :] = earlier[d][...]
        target = d if d == 2 else d + (2 - d) * 2 * place[2]
        o[lead:, :] = hold[lax.rem(f + target, 4)].astype(o.dtype)


def early_sum_body(place, own, both, far, early2, early1, stay, landed, out, cache):
    step = own.shape[0]
    cache[...] = (stay[...].astype(f32) + landed[...].astype(f32)).astype(bf16)
    core = place[2]
    near, other = lag(1, core), lag(3, core)
    out[0] = own[...]
    out[near] = both[:step]
    out[2] = far[...]
    out[other] = both[step:]
    for row, shift in enumerate((0, near, other)):
        rows = slice(row * step, row * step + step)
        r = lax.rem(shift + 2, 4)
        out[r] = out[r] + early2[rows].astype(f32)
        r = lax.rem(shift + near, 4)
        out[r] = out[r] + early1[rows].astype(f32)


def finish_body(place, some, late2, late1, whole, out):
    f, core = place[0], place[2]
    step = some.shape[1]
    for row, (r, more) in enumerate(((lag(3, core), late1), (0, late2), (2, None), (lag(1, core), None))):
        total = some[r] + whole[row * step : row * step + step].astype(f32)
        if more is not None:
            total = total + more[...].astype(f32)
        rows = pl.ds(pl.multiple_of(lax.rem(f + r, 4) * step, step), step)
        out[rows, :] = total.astype(bf16)


def image_body(target, other, rows, sibling, sent, kept):
    step = sent.shape[0]
    for part, out in enumerate((sent, kept)):
        index = part * step + lax.broadcasted_iota(jnp.int32, (step, target.shape[1]), 0)
        hot = jnp.where(index == target[...], 1.0, 0.0).astype(bf16)
        count = target.shape[1]
        total = dot(hot, rows[:count, :])
        hot = jnp.where(index == other[...], 1.0, 0.0).astype(bf16)
        out[...] = (total + dot(hot, sibling[:count, :])).astype(bf16)


def shards(
    hidden,
    lengths,
    page_table,
    first_gain,
    query_weight,
    keyvalue_weight,
    output_weight,
    second_gain,
    gate_weight,
    up_weight,
    down_weight,
):
    tokens, width = hidden.shape
    full = width * 4
    seq_index = lax.axis_index("seq")
    f = lax.axis_index("feat")
    first = seq_index * tokens
    place = jnp.stack([f, first, seq_index % 2]).astype(jnp.int32)
    sds = jax.ShapeDtypeStruct

    x0 = run(copy_body, sds(hidden.shape, bf16), "take_own", [], [hidden])
    x1 = to_side(hidden, (1, 3))
    x2 = from_peer(hidden, 2)
    x3 = to_side(hidden, (3, 1))

    offsets = jnp.cumsum(lengths) - lengths
    ticks = jnp.arange(tokens, dtype=jnp.int32)
    places = jnp.concatenate([first + ticks, first - WIN + ticks, (seq_index ^ 1) * tokens + ticks])
    numbers = jnp.arange(lengths.shape[0], dtype=jnp.int32)
    segment = jnp.sum((places[:, None] >= offsets[None, :]).astype(jnp.int32), axis=1) - 1
    member = (segment[:, None] == numbers[None, :]).astype(jnp.int32)
    inner = places - jnp.sum(member * offsets[None, :], axis=1)
    length = jnp.sum(member * lengths[None, :], axis=1)
    half = HD // 2
    freq = jnp.exp(jnp.arange(half, dtype=f32) * (-2.0 * math.log(10000.0) / HD))
    angle = inner[: 2 * tokens].astype(f32)[:, None] * freq[None, :]
    cosine = jnp.cos(angle)
    sine = jnp.sin(angle)
    cosine = jnp.concatenate([cosine, cosine], axis=1)
    sine = jnp.concatenate([-sine, sine], axis=1)

    pages = page_table.shape[0]
    part_rows = BLK // 4
    keep = inner >= length - WIN
    slot = inner % WIN
    entry = segment * (WIN // BLK) + slot // BLK
    page = jnp.sum(
        jnp.where(
            entry[:, None] == jnp.arange(pages, dtype=jnp.int32)[None, :], page_table[None, :], 0
        ),
        axis=1,
    )
    within = slot % BLK
    owner = page // 2

    def rank(mine, theirs):
        apart = mine ^ theirs
        return jnp.where(apart == 1, 0, jnp.where(apart == 2, 1, jnp.where(apart == 0, 2, 3)))

    column = rank(seq_index // 8, owner // 8) * 4 + rank(seq_index // 2 % 4, owner // 2 % 4)
    mine = keep & (within // part_rows == f) & (owner % 2 == seq_index % 2)
    target = jnp.where(mine, (column * 2 + page % 2) * part_rows + within % part_rows, -1)
    other = target[None, 2 * tokens :]
    target = target[None, :tokens]
    held_rows = 2 * part_rows

    gain1 = first_gain.reshape(4, width)
    gain2 = second_gain.reshape(1, full)
    x1, x3, x2, target, other, cosine, sine, offsets, place, gain1, gain2 = lax.optimization_barrier(
        (x1, x3, x2, target, other, cosine, sine, offsets, place, gain1, gain2)
    )
    step = tokens // 4

    normed, kv_part, kept = run(
        norm_kv_body,
        (
            sds((4, tokens, width), bf16),
            sds((tokens // 2, 128), bf16),
            sds((4, step, width), bf16),
        ),
        "norm_kv",
        [place],
        [x0, x1, x2, x3, gain1, keyvalue_weight],
    )
    far_part = from_earlier(kv_part, 2)
    queries = run(
        query_body,
        sds((tokens, query_weight.shape[1]), bf16),
        "queries",
        [place],
        [normed, query_weight, cosine, sine],
    )
    far_part, queries = lax.optimization_barrier((far_part, queries))
    y0 = run(join_body, sds((tokens, 128), bf16), "join", [], [kv_part, far_part])
    y2, y1, y3 = from_peer(y0, 2), from_peer(y0, 1), from_peer(y0, 3)
    mine = run(
        rotate_body,
        sds((2 * tokens, 2 * HD), bf16),
        "rotate",
        [place],
        [y0, y1, y2, y3, cosine, sine],
        [pltpu.VMEM((4, tokens, 128), f32)],
    )
    theirs = from_partner(mine, 1)
    def halves(rows):
        return [sds((rows.shape[0] // 2, 2 * HD), bf16)] * 2

    def attend(d, kind, cached=()):
        out = sds((step, full), kind)
        return run(
            functools.partial(attend_body, d),
            [out, *halves(cached[0])] if cached else out,
            f"attend{d}",
            [place, offsets],
            [queries, mine, theirs, output_weight, *cached],
            [
                pltpu.VMEM((4 * tokens, 2 * HD), bf16),
                pltpu.VMEM((step, query_weight.shape[1]), bf16),
            ],
        )

    s2 = attend(2, bf16)
    p2 = from_peer(s2, 2)
    image_sent, image_kept = run(
        image_body,
        [sds((8 * held_rows, 2 * HD), bf16)] * 2,
        "image",
        [],
        [target, other, mine, theirs],
    )
    landed = from_partner(image_sent, 8)

    p1 = to_side(attend(1, bf16), (1, 3))
    p3 = to_side(attend(3, bf16), (3, 1))
    p0, stay, go = attend(0, f32, [image_kept, landed])
    landed = from_partner(go, 24)
    residual, normed2, go, stay = run(
        residual_body,
        [sds((4, step, width), f32), sds((step, full), bf16), *halves(stay)],
        "residual",
        [],
        [kept, p0, p1, p2, p3, gain2, stay, landed],
    )
    landed = from_partner(go, 2)
    m1 = to_side(normed2, (1, 3))
    m3 = to_side(normed2, (3, 1))
    hidden_units = gate_weight.shape[1]

    def feed(name, blocks, res=(), before=(), cached=()):
        rows = sum(block.shape[0] for block in blocks)
        lead = {d: rows_before.shape[0] for d, rows_before in before}
        outs = [sds((rows, width), f32)]
        outs += [sds((rows + lead.get(d, 0), width), bf16) for d in (1, 2, 3)]
        more = []
        if cached:
            more = halves(cached[0]) if res else [sds(cached[0].shape, bf16)]
        return run(
            functools.partial(feed_body, len(blocks), bool(res), tuple(lead), len(more)),
            outs + more,
            name,
            [place],
            [*blocks, *cached, *res, *(b for _, b in before), gate_weight, up_weight, down_weight],
            [pltpu.VMEM((rows, hidden_units), bf16), pltpu.VMEM((4, rows, width), f32)],
            vmem=24 << 20,
            flops=20_000_000_000 if len(before) == 3 else 2_000_000_000,
        )

    own0, *own_sent, stay, go = feed("feed_own", [normed2], res=[residual], cached=[stay, landed])
    landed = from_partner(go, 6)
    m1, _ = lax.optimization_barrier((m1, own0))
    m2 = to_side(m1, (1, 3))
    both0, early1, early2, early3 = feed(
        "feed_near", [m1, m3], before=list(zip((1, 2, 3), own_sent))
    )
    early2 = from_peer(early2, 2)
    early1 = to_side(early1, (1, 3))
    far0, late1, late2, whole = feed("feed_far", [m2], before=[(3, early3)])
    whole = to_side(whole, (3, 1))
    late2 = from_peer(late2, 2)
    late1 = to_side(late1, (1, 3))
    some, cache = run(
        early_sum_body,
        [sds((4, step, width), f32), sds((held_rows, 2 * HD), bf16)],
        "early_sum",
        [place],
        [own0, both0, far0, early2, early1, stay, landed],
        flops=10_000_000_000,
    )
    output = run(
        finish_body,
        sds((tokens, width), bf16),
        "finish",
        [place],
        [some, late2, late1, whole],
    )
    return (output, cache.reshape(2, part_rows, 2 * HD))


def solution(mesh):
    placed = (
        P("seq", "feat"),
        P(),
        P(),
        P(),
        P(None, "feat"),
        P(None, "feat"),
        P("feat", None),
        P(),
        P(None, "feat"),
        P(None, "feat"),
        P("feat", None),
    )
    return jax.shard_map(
        shards,
        mesh=mesh,
        in_specs=placed,
        out_specs=(P("seq", "feat"), P("seq", "feat", None)),
        check_vma=False,
    )
```
